32 devices in a mesh: groups: 2 (over x), mp: 8 (over z, y), rows: 2 (over core).
Axes of the slice: x: 2, y: 2, z: 4, core: 2. Of those that a mesh axis runs over, the one named last changes fastest.
Arguments:
- layer_input: bfloat16 [1536, 5120], P(('groups', 'rows')), parts along dimension 0, may hold values from -6 to 6
- norm_gain: float32 [5120], replicated, may hold values from 0.5 to 1.5
- norm_bias: float32 [5120], replicated, may hold values from -1.5 to 1.5
- w_query_key: bfloat16 [2, 5120, 4096], P(None, None, 'mp'), may hold values from -1 to 1
- w_value: bfloat16 [5120, 4096], P(None, 'mp'), may hold values from -0.078125 to 0.078125
- w_out: bfloat16 [4096, 5120], P('mp'), may hold values from -0.75 to 0.75
- w_maps: bfloat16 [32, 128], replicated, may hold values from -1 to 1
- b_maps: float32 [128], replicated, may hold values from -3 to 3
- pair_gain: float32 [128], replicated, may hold values from 0.5 to 1.5
- pair_bias: float32 [128], replicated, may hold values from -3 to 3
- w_up: bfloat16 [128, 512], replicated, may hold values from -0.5 to 0.5
- b_up: float32 [512], replicated, may hold values from -3 to 3
- w_down: bfloat16 [512, 128], replicated, may hold values from -0.25 to 0.25
- b_down: float32 [128], replicated, may hold values from -3 to 3
Outputs:
- attention: float32 [1536, 5120], P(('groups', 'rows'), 'mp'), parts along dimension 0
- pair_features: bfloat16 [1536, 768, 128], P(('groups', 'rows'), 'mp'), parts along dimension 0
The draws below stay inside these ranges and needn't reach their ends.
There are 2 independent parts, one for each index of `groups`. The reference program is written for one: setup_inputs(seed, part) draws one part's arguments, and reference() takes and returns one part's arrays. A program takes and returns all parts, laid end to end along the dimension named above; an argument that names none is the same for every part. Nothing has to cross between parts.
All inputs are finite; a program needn't handle non-finite values.
Results may differ from the reference program's by a relative error of at most 0.0055.
The reference program's roundings to bfloat16 on the way count: a program that leaves them out, or rounds other values in their place, can miss the bound.
Values may be sent and summed in bfloat16 or wider, within the bound.
No kernel may reach another device: no remote copies, remote signals or barrier semaphores. Data moves between devices by JAX's collectives and lax.ppermute only.
A program may use at most 192 MiB of HBM per device.

```python
import math
import jax
import jax.numpy as jnp
from jax import lax

D = 5120
HD = 128
HEADS = 32
PAIR = 128
TRANS = 512
TOKENS = 768


def bias_vector(key):
    seed_bias = jax.random.fold_in(key, 7)
    return jnp.clip(0.5 * jax.random.normal(seed_bias, (D,), jnp.float32), -1.5, 1.5)


def draw_norm_bias(key, part):
    return bias_vector(key)


def draw_w_query_key(key, part):
    seed_query, seed_keys = jax.random.split(key, 2)
    width_all = HEADS * HD
    queries = jax.random.normal(seed_query, (D, width_all), jnp.float32) / math.sqrt(D)
    keys_weight = jax.random.normal(seed_keys, (D, width_all), jnp.float32) / math.sqrt(D)
    queries = jnp.clip(queries, -1.0, 1.0)
    keys_weight = jnp.clip(keys_weight, -1.0, 1.0)
    return jnp.stack([queries, keys_weight]).astype(jnp.bfloat16)


def levels(rng, shape, cuts, low, top_value):
    factor_of, own = 1.0, jax.random.fold_in(rng, 6)
    for dim, parts in cuts:
        draws = jnp.exp(jax.random.uniform(jax.random.fold_in(own, dim), (parts,), jnp.float32, low / len(cuts), top_value / len(cuts)))
        factor_of = factor_of * jnp.repeat(draws, shape[dim] // parts).reshape([-1 if axis == dim else 1 for axis in range(len(shape))])
    return factor_of


def noise(stream_key, extent, deviation, reach, cuts=(), kind=jnp.bfloat16):
    array = jax.random.normal(stream_key, extent, jnp.float32) * deviation
    if len(cuts) > 0:
        array = levels(stream_key, extent, cuts, -0.22, 0.18) * array
    return jnp.clip(array, min=-reach, max=reach).astype(kind)


def setup_inputs(seed: int = 0, part: int = 0) -> dict:
    seeds = jax.random.split(jax.random.key(seed), 15)
    part_keys = jax.random.split(jax.random.fold_in(seeds[14], part), 15)
    return {
        "layer_input": noise(part_keys[0], (TOKENS, D), 1.0, 6.0, ((0, 2),)),
        "norm_gain": jnp.clip(1.0 + 0.1 * jax.random.normal(seeds[1], (D,), jnp.float32), 0.5, 1.5),
        "norm_bias": draw_norm_bias(jax.random.fold_in(seeds[14], 71), part),
        "w_query_key": draw_w_query_key(jax.random.fold_in(seeds[14], 71), part),
        "w_value": noise(seeds[4], (D, HEADS * HD), D ** -0.5, 0.078125, ((1, 8),)),
        "w_out": noise(seeds[5], (HEADS * HD, D), (HEADS * HD // 64) ** -0.5, 0.75, ((0, 8),)),
        "w_maps": noise(seeds[6], (HEADS, PAIR), HEADS ** -0.5, 1.0),
        "b_maps": noise(seeds[7], (PAIR,), 0.5, 3.0, (), jnp.float32),
        "pair_gain": jnp.clip(1.0 + 0.1 * jax.random.normal(seeds[8], (PAIR,), jnp.float32), 0.5, 1.5),
        "pair_bias": noise(seeds[9], (PAIR,), 0.5, 3.0, (), jnp.float32),
        "w_up": noise(seeds[10], (PAIR, TRANS), PAIR ** -0.5, 0.5),
        "b_up": noise(seeds[11], (TRANS,), 0.5, 3.0, (), jnp.float32),
        "w_down": noise(seeds[12], (TRANS, PAIR), TRANS ** -0.5, 0.25),
        "b_down": noise(seeds[13], (PAIR,), 0.5, 3.0, (), jnp.float32),
    }


def layer_norm(values, gain, bias):
    average = lax.optimization_barrier(jnp.mean(values, axis=-1, keepdims=True))
    centered = values - average
    variance = lax.optimization_barrier(jnp.mean(centered * centered, axis=-1, keepdims=True))
    return centered * lax.rsqrt(variance + 1e-05) * gain + bias

def rotate(values, positions):
    half = values.shape[-1] // 2
    freqs = 10000.0 ** (-jnp.arange(half, dtype=jnp.float32) / half)
    angles = positions.astype(jnp.float32)[:, None] * freqs[None, :]
    cosine = jnp.cos(angles)[:, None, :]
    sine = jnp.sin(angles)[:, None, :]
    lower = values[..., :half]
    upper = values[..., half:]
    return jnp.concatenate([lower * cosine - upper * sine, upper * cosine + lower * sine], axis=-1)

def pair_block(maps, w_maps, b_maps, pair_gain, pair_bias, w_up, b_up, w_down, b_down):
    mixed = jnp.einsum('hrc,hp->rcp', maps.astype(jnp.float32), w_maps.astype(jnp.float32)) * TOKENS + b_maps
    normed = layer_norm(mixed, pair_gain, pair_bias).astype(jnp.bfloat16)
    hidden = jax.nn.relu(jnp.einsum('rcp,pt->rct', normed.astype(jnp.float32), w_up.astype(jnp.float32)) + b_up).astype(jnp.bfloat16)
    return (jnp.einsum('rct,tp->rcp', hidden.astype(jnp.float32), w_down.astype(jnp.float32)) + b_down).astype(jnp.bfloat16)

def reference(layer_input, norm_gain, norm_bias, w_query_key, w_value, w_out, w_maps, b_maps, pair_gain, pair_bias, w_up, b_up, w_down, b_down):
    normed = layer_norm(layer_input.astype(jnp.float32), norm_gain, norm_bias).astype(jnp.bfloat16)
    positions = jnp.arange(TOKENS, dtype=jnp.int32)
    queries = jnp.dot(normed, w_query_key[0], preferred_element_type=jnp.float32).reshape(TOKENS, HEADS, HD)
    queries = rotate(queries, positions).astype(jnp.bfloat16)
    keys_all = jnp.dot(normed, w_query_key[1], preferred_element_type=jnp.float32).reshape(TOKENS, HEADS, HD)
    keys_all = rotate(keys_all, positions).astype(jnp.bfloat16)
    values_all = jnp.dot(normed, w_value, preferred_element_type=jnp.float32).astype(jnp.bfloat16).reshape(TOKENS, HEADS, HD)

    def one_head(operands):
        head_queries, head_keys, head_values = operands
        scores = jnp.dot(head_queries, head_keys.T, preferred_element_type=jnp.float32) / math.sqrt(HD)
        weights = jax.nn.softmax(scores, axis=-1).astype(jnp.bfloat16)
        context = jnp.dot(weights, head_values, preferred_element_type=jnp.float32).astype(jnp.bfloat16)
        return (weights, context)
    maps, context = lax.map(one_head, (queries.transpose(1, 0, 2), keys_all.transpose(1, 0, 2), values_all.transpose(1, 0, 2)))
    context = context.transpose(1, 0, 2).reshape(TOKENS, HEADS * HD)
    attention = jnp.dot(context, w_out, preferred_element_type=jnp.float32)
    grouped = maps.reshape(HEADS, TOKENS // 16, 16, TOKENS).transpose(1, 0, 2, 3)
    pairs = lax.map(lambda piece: pair_block(piece, w_maps, b_maps, pair_gain, pair_bias, w_up, b_up, w_down, b_down), grouped)
    return (attention, pairs.reshape(TOKENS, TOKENS, PAIR))
```

```python
import functools
import math

import jax
import jax.numpy as jnp
from jax import lax
from jax.experimental import pallas as pl
from jax.experimental.pallas import tpu as pltpu
from jax.sharding import PartitionSpec as P

HD = 128
F32 = jnp.float32
BF16 = jnp.bfloat16
ROOT = math.sqrt(HD)
VMEM_LIMIT = 60 * 1024 * 1024


def params(*axes):
    return pltpu.CompilerParams(
        dimension_semantics=axes if axes else None, vmem_limit_bytes=VMEM_LIMIT
    )


def cost(flops, moved, transcendentals=0):
    return pl.CostEstimate(
        flops=int(flops), bytes_accessed=int(moved), transcendentals=int(transcendentals)
    )


def sds(shape, dtype):
    return jax.ShapeDtypeStruct(shape, dtype)


def turn(block, cosine, sine):
    pieces = []
    for head in range(block.shape[1] // HD):
        one = block[:, head * HD : (head + 1) * HD]
        pieces.append(one * cosine + pltpu.roll(one, HD // 2, 1) * sine)
    return jnp.concatenate(pieces, axis=1)


def norm_keys_kernel(x_ref, gain_ref, bias_ref, w_ref, cos_ref, sin_ref, normed_ref, out_ref):
    rows, width = x_ref.shape
    step = 16

    @pl.when(pl.program_id(0) == 0)
    def _():
        def body(i, carry):
            at = pl.ds(pl.multiple_of(i * step, step), step)
            x = x_ref[at, :].astype(F32)
            centered = x - jnp.sum(x, axis=1, keepdims=True) * (1.0 / width)
            variance = jnp.sum(centered * centered, axis=1, keepdims=True) * (1.0 / width)
            scaled = centered * lax.rsqrt(variance + 1e-05)
            normed_ref[at, :] = (scaled * gain_ref[...] + bias_ref[...]).astype(BF16)
            return carry

        lax.fori_loop(0, rows // step, body, 0)

    block = jnp.dot(normed_ref[...], w_ref[0], preferred_element_type=F32)
    out_ref[...] = turn(block, cos_ref[...], sin_ref[...]).astype(BF16)


def norm_keys(x, gain, bias, w, cosine, sine, tile=256):
    rows, width = x.shape
    columns = w.shape[2]
    return pl.pallas_call(
        norm_keys_kernel,
        grid=(columns // tile,),
        in_specs=[
            pl.BlockSpec((rows, width), lambda n: (0, 0)),
            pl.BlockSpec((1, width), lambda n: (0, 0)),
            pl.BlockSpec((1, width), lambda n: (0, 0)),
            pl.BlockSpec((1, width, tile), lambda n: (1, 0, n)),
            pl.BlockSpec((rows, HD), lambda n: (0, 0)),
            pl.BlockSpec((rows, HD), lambda n: (0, 0)),
        ],
        out_specs=[
            pl.BlockSpec((rows, width), lambda n: (0, 0)),
            pl.BlockSpec((rows, tile), lambda n: (0, n)),
        ],
        out_shape=[sds((rows, width), BF16), sds((rows, columns), BF16)],
        compiler_params=params("arbitrary"),
        cost_estimate=cost(2 * rows * width * columns, 2 * width * (2 * rows + columns)),
        name="norm_keys",
    )(x, gain.reshape(1, width), bias.reshape(1, width), w, cosine, sine)


def queries_kernel(normed_ref, w_ref, cos_ref, sin_ref, out_ref):
    block = jnp.dot(normed_ref[...], w_ref[0], preferred_element_type=F32)
    out_ref[...] = turn(block, cos_ref[...], sin_ref[...]).astype(BF16)


def project_queries(normed, w, cosine, sine, tile=256):
    rows, width = normed.shape
    columns = w.shape[2]
    return pl.pallas_call(
        queries_kernel,
        grid=(columns // tile,),
        in_specs=[
            pl.BlockSpec((rows, width), lambda n: (0, 0)),
            pl.BlockSpec((1, width, tile), lambda n: (0, 0, n)),
            pl.BlockSpec((rows, HD), lambda n: (0, 0)),
            pl.BlockSpec((rows, HD), lambda n: (0, 0)),
        ],
        out_specs=pl.BlockSpec((rows, tile), lambda n: (0, n)),
        out_shape=sds((rows, columns), BF16),
        compiler_params=params("arbitrary"),
        cost_estimate=cost(2 * rows * width * columns, 2 * width * (rows + columns)),
        name="project_queries",
    )(normed, w, cosine, sine)


def values_kernel(normed_ref, w_ref, out_ref):
    out_ref[...] = jnp.dot(normed_ref[...], w_ref[...], preferred_element_type=F32).astype(BF16)


def project_values(normed, w, tile=256):
    rows, width = normed.shape
    columns = w.shape[1]
    return pl.pallas_call(
        values_kernel,
        grid=(columns // tile,),
        in_specs=[
            pl.BlockSpec((rows, width), lambda n: (0, 0)),
            pl.BlockSpec((width, tile), lambda n: (0, n)),
        ],
        out_specs=pl.BlockSpec((rows, tile), lambda n: (0, n)),
        out_shape=sds((rows, columns), BF16),
        compiler_params=params("arbitrary"),
        cost_estimate=cost(2 * rows * width * columns, 2 * width * (rows + columns)),
        name="project_values",
    )(normed, w)


def softmax_kernel(q_ref, k_ref, maps_ref, packet_ref):
    rows, width = q_ref.shape
    heads = width // HD
    lane = lax.broadcasted_iota(jnp.int32, (rows, HD), 1)
    table = jnp.zeros((rows, HD), F32)
    for head in range(heads):
        at = slice(head * HD, (head + 1) * HD)
        scores = lax.dot_general(
            q_ref[:, at], k_ref[:, at], (((1,), (1,)), ((), ())), preferred_element_type=F32
        ) * (1.0 / ROOT)
        top = jnp.max(scores, axis=1, keepdims=True)
        raised = jnp.exp(scores - top)
        total = jnp.sum(raised, axis=1, keepdims=True)
        maps_ref[head] = (raised * (1.0 / total)).astype(BF16)
        level = (top + jnp.log(total)) * ROOT
        high = level.astype(BF16).astype(F32)
        middle = (level - high).astype(BF16).astype(F32)
        low = (level - high - middle).astype(BF16).astype(F32)
        for piece, part in enumerate((high, middle, low)):
            table = jnp.where(lane == 3 * head + piece, part, table)
    packet_ref[0:rows, :] = q_ref[...]
    packet_ref[rows : rows + 16, :] = jnp.zeros((16, width), BF16)
    packet_ref[rows : rows + 16, 0:rows] = table.T[0:16].astype(BF16)


def softmax_maps(queries, keys):
    rows, width = queries.shape
    tokens = keys.shape[0]
    heads = width // HD
    return pl.pallas_call(
        softmax_kernel,
        out_shape=[sds((heads, rows, tokens), BF16), sds((rows + 16, width), BF16)],
        in_specs=[pl.BlockSpec(memory_space=pltpu.VMEM)] * 2,
        out_specs=[pl.BlockSpec(memory_space=pltpu.VMEM)] * 2,
        compiler_params=params(),
        cost_estimate=cost(2 * rows * tokens * width, 2 * heads * rows * tokens, heads * rows * tokens),
        name="softmax_maps",
    )(queries, keys)


def context_kernel(maps_ref, v_ref, out_ref):
    for head in range(maps_ref.shape[0]):
        at = slice(head * HD, (head + 1) * HD)
        out_ref[:, at] = jnp.dot(
            maps_ref[head], v_ref[:, at], preferred_element_type=F32
        ).astype(BF16)


def context_of(maps, values):
    heads, rows, tokens = maps.shape
    return pl.pallas_call(
        context_kernel,
        out_shape=sds((rows, heads * HD), BF16),
        in_specs=[pl.BlockSpec(memory_space=pltpu.VMEM)] * 2,
        out_specs=pl.BlockSpec(memory_space=pltpu.VMEM),
        compiler_params=params(),
        cost_estimate=cost(2 * heads * rows * tokens * HD, 2 * heads * rows * tokens),
        name="context",
    )(maps, values)


def project_out_kernel(count, order_ref, context_ref, w_ref, *out_refs):
    block = jnp.dot(context_ref[...], w_ref[...], preferred_element_type=F32)
    for place in range(count):

        @pl.when(pl.program_id(0) == place)
        def _(place=place):
            out_refs[place][...] = block.astype(out_refs[place].dtype)


def project_out(context, w, order, dtype):
    rows, depth = context.shape
    count = order.shape[0]
    tile = w.shape[1] // (2 * count)
    return pl.pallas_call(
        functools.partial(project_out_kernel, count),
        grid_spec=pltpu.PrefetchScalarGridSpec(
            num_scalar_prefetch=1,
            grid=(count,),
            in_specs=[
                pl.BlockSpec((rows, depth), lambda n, order: (0, 0)),
                pl.BlockSpec((depth, tile), lambda n, order: (0, order[n])),
            ],
            out_specs=[pl.BlockSpec((rows, tile), lambda n, order: (0, 0))] * count,
        ),
        out_shape=[sds((rows, tile), dtype)] * count,
        compiler_params=params("arbitrary"),
        cost_estimate=cost(2 * rows * depth * tile * count, 2 * count * tile * (rows + depth)),
        name="project_out",
    )(order, context, w)


def pair_maps_kernel(packet_ref, k_ref, own_ref, other_ref):
    rows = own_ref.shape[0]
    width = packet_ref.shape[1]
    heads = width // HD
    columns = k_ref.shape[1]
    lane_head = lax.broadcasted_iota(jnp.int32, (columns, width), 1) // HD
    wide = heads * columns
    row = lax.broadcasted_iota(jnp.int32, (16, wide), 0)
    column = lax.broadcasted_iota(jnp.int32, (16, wide), 1)
    hit = jnp.zeros((16, wide), jnp.bool_)
    for head in range(heads):
        inside = (column >= head * columns) & (column < (head + 1) * columns)
        hit = hit | (inside & (row >= 3 * head) & (row < 3 * head + 3))
    pick = jnp.where(hit, -1.0, 0.0).astype(BF16)
    level = lax.dot_general(
        packet_ref[rows : rows + 16, 0:rows],
        pick,
        (((0,), (0,)), ((), ())),
        preferred_element_type=F32,
    )
    for place, out_ref in enumerate((own_ref, other_ref)):
        k = k_ref[place].astype(F32)
        spread = jnp.concatenate(
            [jnp.where(lane_head == head, k, 0.0) for head in range(heads)], axis=0
        ).astype(BF16)
        scores = lax.dot_general(
            packet_ref[0:rows, :], spread, (((1,), (1,)), ((), ())), preferred_element_type=F32
        )
        out_ref[...] = jnp.exp((scores + level) * (1.0 / ROOT)).astype(BF16)


def pair_maps(packet, keys):
    rows, width = packet.shape[0] - 16, packet.shape[1]
    wide = (width // HD) * keys.shape[1]
    return pl.pallas_call(
        pair_maps_kernel,
        out_shape=[sds((rows, wide), BF16)] * 2,
        in_specs=[pl.BlockSpec(memory_space=pltpu.VMEM)] * 2,
        out_specs=[pl.BlockSpec(memory_space=pltpu.VMEM)] * 2,
        compiler_params=params(),
        cost_estimate=cost(4 * rows * wide * width, 8 * rows * wide, 2 * rows * wide),
        name="pair_maps",
    )(packet, keys)


def pair_kernel(factor, count, *refs):
    maps_refs = refs[:count]
    (w_maps_ref, b_maps_ref, gain_ref, bias_ref, w_up_ref, b_up_ref, w_down_ref, b_down_ref) = refs[
        count : count + 8
    ]
    out_ref, spread_ref, ones_ref, shift_ref, rows_ref = refs[count + 8 :]
    block = out_ref.shape[0]
    columns = out_ref.shape[1]
    channels = out_ref.shape[2]
    heads_all = w_maps_ref.shape[0]
    heads = heads_all // count
    group = HD // heads_all

    @pl.when(pl.program_id(0) == 0)
    def _():
        w = w_maps_ref[...].astype(F32)
        w = (w - jnp.sum(w, axis=1, keepdims=True) * (1.0 / channels)) * factor
        high = w.astype(BF16)
        low = (w - high.astype(F32)).astype(BF16)
        spread_ref[...] = jnp.zeros_like(spread_ref)
        for i in range(group):
            at = slice(i * channels, (i + 1) * channels)
            spread_ref[i * heads_all : (i + 1) * heads_all, at] = high
            spread_ref[HD + i * heads_all : HD + (i + 1) * heads_all, at] = low
        b = b_maps_ref[...]
        b = b - jnp.sum(b, axis=1, keepdims=True) * (1.0 / channels)
        shift_ref[...] = jnp.concatenate([b] * group, axis=1)
        a = lax.broadcasted_iota(jnp.int32, ones_ref.shape, 0) // channels
        c = lax.broadcasted_iota(jnp.int32, ones_ref.shape, 1) // channels
        ones_ref[...] = jnp.where(a == c, 1.0 / channels, 0.0).astype(BF16)
        rows_ref[...] = jnp.zeros_like(rows_ref)

    for source in range(count):
        wide = maps_refs[source][...].astype(F32)
        for head in range(heads):
            place = (source * heads + head) * block
            rows_ref[place : place + block, 0:columns] = wide[
                :, head * columns : (head + 1) * columns
            ]
    gain = jnp.concatenate([gain_ref[...]] * group, axis=1)
    bias = jnp.concatenate([bias_ref[...]] * group, axis=1)
    for g in range(block // group):
        tall = jnp.concatenate(
            [rows_ref[pl.ds(g * group + i, heads_all, stride=block), :] for i in range(group)], axis=0
        )
        flat = tall.T[0:columns].astype(BF16)
        centered = (
            jnp.dot(
                jnp.concatenate([flat, flat], axis=1), spread_ref[...], preferred_element_type=F32
            )
            + shift_ref[...]
        )
        square = (centered * centered).astype(BF16)
        half = ones_ref.shape[0]
        variance = jnp.concatenate(
            [
                jnp.dot(square[:, at : at + half], ones_ref[...], preferred_element_type=F32)
                for at in range(0, group * channels, half)
            ],
            axis=1,
        )
        normed = (centered * lax.rsqrt(variance + 1e-05) * gain + bias).astype(BF16)
        stacked = jnp.concatenate(
            [normed[:, i * channels : (i + 1) * channels] for i in range(group)], axis=0
        )
        hidden = jnp.dot(stacked, w_up_ref[...], preferred_element_type=F32) + b_up_ref[...]
        hidden = jnp.maximum(hidden, 0.0).astype(BF16)
        result = jnp.dot(hidden, w_down_ref[...], preferred_element_type=F32) + b_down_ref[...]
        result = result.astype(BF16)
        for i in range(group):
            out_ref[g * group + i] = result[i * columns : (i + 1) * columns]


def pair_block_fast(
    maps, w_maps, b_maps, pair_gain, pair_bias, w_up, b_up, w_down, b_down, factor, columns, block=16
):
    count = len(maps)
    rows, wide = maps[0].shape
    channels, hidden = w_up.shape
    heads_all = w_maps.shape[0]
    group = HD // heads_all
    whole = lambda *shape: pl.BlockSpec(shape, lambda n: (0,) * len(shape))
    pairs = rows * columns
    return pl.pallas_call(
        functools.partial(pair_kernel, factor, count),
        grid=(rows // block,),
        in_specs=[pl.BlockSpec((block, wide), lambda n: (n, 0))] * count
        + [
            whole(heads_all, channels),
            whole(1, channels),
            whole(1, channels),
            whole(1, channels),
            whole(channels, hidden),
            whole(1, hidden),
            whole(hidden, channels),
            whole(1, channels),
        ],
        out_specs=pl.BlockSpec((block, columns, channels), lambda n: (n, 0, 0)),
        out_shape=sds((rows, columns, channels), BF16),
        scratch_shapes=[
            pltpu.VMEM((2 * HD, group * channels), BF16),
            pltpu.VMEM((2 * channels, 2 * channels), BF16),
            pltpu.VMEM((1, group * channels), F32),
            pltpu.VMEM((heads_all * block, HD), F32),
        ],
        compiler_params=params("arbitrary"),
        cost_estimate=cost(4 * pairs * channels * hidden, 4 * pairs * channels, pairs * channels),
        name="pair_block",
    )(
        *maps,
        w_maps,
        b_maps.reshape(1, -1),
        pair_gain.reshape(1, -1),
        pair_bias.reshape(1, -1),
        w_up,
        b_up.reshape(1, -1),
        w_down,
        b_down.reshape(1, -1),
    )


def per_device_fast(
    layer_input,
    norm_gain,
    norm_bias,
    w_query_key,
    w_value,
    w_out,
    w_maps,
    b_maps,
    pair_gain,
    pair_bias,
    w_up,
    b_up,
    w_down,
    b_down,
):
    rows = layer_input.shape[0]
    parts = lax.axis_size("mp")
    ring = parts // 2
    tokens = rows * lax.axis_size("rows")
    columns = tokens // parts
    heads = w_value.shape[1] // HD
    core = lax.axis_index("rows")
    z, y = lax.axis_index("mp") // 2, lax.axis_index("mp") % 2

    swap_core = [(0, 1), (1, 0)]
    swap_y = [(m, m ^ 1) for m in range(parts)]

    def rotate_z(by):
        return [(2 * a + b, 2 * ((a + by) % ring) + b) for a in range(ring) for b in range(2)]

    half = HD // 2
    freqs = 10000.0 ** (-jnp.arange(half, dtype=F32) / half)
    positions = core * rows + jnp.arange(rows, dtype=jnp.int32)
    angles = positions.astype(F32)[:, None] * freqs[None, :]
    cosine, sine = jnp.cos(angles), jnp.sin(angles)
    cosine = jnp.concatenate([cosine, cosine], axis=1)
    sine = jnp.concatenate([-sine, sine], axis=1)

    normed, keys = norm_keys(layer_input, norm_gain, norm_bias, w_query_key, cosine, sine)
    keys_there = lax.ppermute(keys, "rows", swap_core)
    queries = project_queries(normed, w_query_key, cosine, sine)
    first = core == 0
    keys_all = jnp.concatenate(
        [jnp.where(first, keys, keys_there), jnp.where(first, keys_there, keys)], axis=0
    )
    maps, packet = softmax_maps(queries, keys_all)
    packets = [packet]
    packets.append(lax.ppermute(packet, "mp", rotate_z(1)))

    shares = lax.dynamic_index_in_dim(
        keys_all.reshape(ring, 2, columns, -1), core, axis=1, keepdims=False
    )
    share = [lax.dynamic_index_in_dim(shares, (z + d) % ring, 0, keepdims=False) for d in range(ring)]
    mine = jnp.stack(
        [share[0]] + [lax.ppermute(share[d], "mp", rotate_z(d)) for d in range(1, ring)]
    )
    theirs = lax.ppermute(mine, "rows", swap_core)
    here = y == core
    key_columns = jnp.stack([jnp.where(here, mine, theirs), jnp.where(here, theirs, mine)], axis=1)

    values = project_values(normed, w_value)
    values_there = lax.ppermute(values, "rows", swap_core)

    own_maps, other_maps = [], []
    for d in range(ring):
        if d >= 2:
            packets.append(lax.ppermute(packets[-1], "mp", rotate_z(1)))
        own, other = pair_maps(packets[d], key_columns[d])
        own_maps.append(own)
        other_maps.append(lax.ppermute(other, "mp", swap_y))

    values_all = jnp.concatenate(
        [jnp.where(first, values, values_there), jnp.where(first, values_there, values)], axis=0
    )
    context = context_of(maps, values_all)
    order = 2 * ((z - 1 - jnp.arange(ring, dtype=jnp.int32)) % ring)
    away = project_out(context, w_out, order + 1 - y, BF16)
    home = project_out(context, w_out, order + y, F32)
    running = None
    for d in range(ring):
        arrived = lax.ppermute(away[d], "mp", swap_y)
        total = home[d] + arrived.astype(F32)
        if running is not None:
            total = total + running.astype(F32)
        if d < ring - 1:
            running = lax.ppermute(total.astype(BF16), "mp", rotate_z(1))
    attention = total

    source = (z - jnp.arange(ring, dtype=jnp.int32)) % ring
    head_order = jnp.concatenate([2 * source + y, 2 * source + 1 - y])
    w_sorted = w_maps.reshape(parts, heads, -1)[head_order].reshape(w_maps.shape)
    pair_features = pair_block_fast(
        own_maps + other_maps,
        w_sorted,
        b_maps,
        pair_gain,
        pair_bias,
        w_up,
        b_up,
        w_down,
        b_down,
        float(tokens),
        columns,
    )
    return (attention, pair_features)


def layer_norm(values, gain, bias):
    average = jnp.mean(values, axis=-1, keepdims=True)
    centered = values - average
    variance = jnp.mean(centered * centered, axis=-1, keepdims=True)
    return centered * lax.rsqrt(variance + 1e-05) * gain + bias


def rotate(values, positions):
    half = values.shape[-1] // 2
    freqs = 10000.0 ** (-jnp.arange(half, dtype=jnp.float32) / half)
    angles = positions.astype(jnp.float32)[:, None] * freqs[None, :]
    cosine = jnp.cos(angles)[:, None, :]
    sine = jnp.sin(angles)[:, None, :]
    lower = values[..., :half]
    upper = values[..., half:]
    return jnp.concatenate([lower * cosine - upper * sine, upper * cosine + lower * sine], axis=-1)


def project_rotated(normed, weight, positions):
    count = normed.shape[0]
    projected = jnp.dot(normed, weight, preferred_element_type=jnp.float32)
    projected = projected.reshape(count, weight.shape[1] // HD, HD)
    return rotate(projected, positions).astype(jnp.bfloat16).reshape(count, weight.shape[1])


def pair_block(maps, w_maps, b_maps, pair_gain, pair_bias, w_up, b_up, w_down, b_down, factor):
    mixed = (
        jnp.einsum("hrc,hp->rcp", maps, w_maps, preferred_element_type=jnp.float32) * factor
        + b_maps
    )
    normed = layer_norm(mixed, pair_gain, pair_bias).astype(jnp.bfloat16)
    hidden = jax.nn.relu(
        jnp.einsum("rcp,pt->rct", normed, w_up, preferred_element_type=jnp.float32) + b_up
    ).astype(jnp.bfloat16)
    return (
        jnp.einsum("rct,tp->rcp", hidden, w_down, preferred_element_type=jnp.float32) + b_down
    ).astype(jnp.bfloat16)


def per_device(
    layer_input,
    norm_gain,
    norm_bias,
    w_query_key,
    w_value,
    w_out,
    w_maps,
    b_maps,
    pair_gain,
    pair_bias,
    w_up,
    b_up,
    w_down,
    b_down,
):
    tok_rows = layer_input.shape[0]
    tokens_all = tok_rows * lax.axis_size("rows")
    local_heads = w_value.shape[1] // HD
    normed = layer_norm(layer_input.astype(jnp.float32), norm_gain, norm_bias).astype(jnp.bfloat16)
    own_positions = lax.axis_index("rows") * tok_rows + jnp.arange(tok_rows, dtype=jnp.int32)
    queries = project_rotated(normed, w_query_key[0], own_positions)
    keys_local = project_rotated(normed, w_query_key[1], own_positions)
    values_local = jnp.dot(normed, w_value, preferred_element_type=jnp.float32).astype(jnp.bfloat16)
    keys_all, values_all = (
        lax.all_gather(keys_local, "rows", axis=0, tiled=True),
        lax.all_gather(values_local, "rows", axis=0, tiled=True),
    )
    head_queries = queries.reshape(tok_rows, local_heads, HD)
    head_keys = keys_all.reshape(tokens_all, local_heads, HD)
    head_values = values_all.reshape(tokens_all, local_heads, HD)
    scores = jnp.einsum(
        "qhd,khd->hqk", head_queries, head_keys, preferred_element_type=jnp.float32
    ) / math.sqrt(HD)
    maps = jax.nn.softmax(scores, axis=-1).astype(jnp.bfloat16)
    context = jnp.einsum("hqk,khd->qhd", maps, head_values, preferred_element_type=jnp.float32)
    context = context.astype(jnp.bfloat16).reshape(tok_rows, local_heads * HD)
    partial_sums = jnp.dot(context, w_out, preferred_element_type=jnp.float32)
    attention = lax.psum_scatter(partial_sums, "mp", scatter_dimension=1, tiled=True)
    factor = float(tokens_all)
    pair_features = pair_block(
        lax.all_to_all(maps, "mp", split_axis=2, concat_axis=0, tiled=True),
        w_maps,
        b_maps,
        pair_gain,
        pair_bias,
        w_up,
        b_up,
        w_down,
        b_down,
        factor,
    )
    return (attention, pair_features)


def solution(mesh):
    in_specs = (
        P(("groups", "rows"), None),
        P(),
        P(),
        P(None, None, "mp"),
        P(None, "mp"),
        P("mp", None),
        P(),
        P(),
        P(),
        P(),
        P(),
        P(),
        P(),
        P(),
    )
    out_specs = (P(("groups", "rows"), "mp"), P(("groups", "rows"), "mp", None))
    small = mesh.shape["mp"] == 8 and mesh.shape["rows"] == 2
    return jax.shard_map(
        per_device_fast if small else per_device, mesh=mesh, in_specs=in_specs, out_specs=out_specs, check_vma=False
    )
```

```python
import functools
import math

import jax
import jax.numpy as jnp
from jax import lax
from jax.experimental import pallas as pl
from jax.experimental.pallas import tpu as pltpu
from jax.sharding import PartitionSpec as P

HD = 128
F32 = jnp.float32
BF16 = jnp.bfloat16
ROOT = math.sqrt(HD)
VMEM_LIMIT = 60 * 1024 * 1024


def params(*axes):
    return pltpu.CompilerParams(
        dimension_semantics=axes if axes else None, vmem_limit_bytes=VMEM_LIMIT
    )


def cost(flops, moved, transcendentals=0):
    return pl.CostEstimate(
        flops=int(flops), bytes_accessed=int(moved), transcendentals=int(transcendentals)
    )


def sds(shape, dtype):
    return jax.ShapeDtypeStruct(shape, dtype)


def turn(block, cosine, sine):
    pieces = []
    for head in range(block.shape[1] // HD):
        one = block[:, head * HD : (head + 1) * HD]
        pieces.append(one * cosine + pltpu.roll(one, HD // 2, 1) * sine)
    return jnp.concatenate(pieces, axis=1)


def keys_queries_kernel(
    x_ref, gain_ref, bias_ref, w_ref, cos_ref, sin_ref, normed_ref, k_ref, q_ref, w_vmem, sems
):
    rows, width = x_ref.shape
    columns = k_ref.shape[1]
    step = 16
    copies = [
        pltpu.make_async_copy(w_ref.at[which], w_vmem.at[which], sems.at[which]) for which in (1, 0)
    ]
    for copy in copies:
        copy.start()

    def body(i, carry):
        at = pl.ds(pl.multiple_of(i * step, step), step)
        total = jnp.zeros((step, HD), F32)
        for n in range(width // HD):
            total = total + x_ref[at, n * HD : (n + 1) * HD].astype(F32)
        mean = jnp.sum(total, axis=1, keepdims=True) * (1.0 / width)
        total = jnp.zeros((step, HD), F32)
        for n in range(width // HD):
            centered = x_ref[at, n * HD : (n + 1) * HD].astype(F32) - mean
            total = total + centered * centered
        variance = jnp.sum(total, axis=1, keepdims=True) * (1.0 / width)
        scale = lax.rsqrt(variance + 1e-05)
        for n in range(width // HD):
            lanes = slice(n * HD, (n + 1) * HD)
            scaled = (x_ref[at, lanes].astype(F32) - mean) * scale
            normed_ref[at, lanes] = (scaled * gain_ref[:, lanes] + bias_ref[:, lanes]).astype(BF16)
        return carry

    lax.fori_loop(0, rows // step, body, 0)
    tile = min(256, columns)
    for copy, which, out_ref in zip(copies, (1, 0), (k_ref, q_ref)):
        copy.wait()
        for n in range(0, columns, tile):
            block = jnp.dot(
                normed_ref[...], w_vmem[which, :, n : n + tile], preferred_element_type=F32
            )
            out_ref[:, n : n + tile] = turn(block, cos_ref[...], sin_ref[...]).astype(BF16)


def keys_queries(x, gain, bias, w, cosine, sine):
    rows, width = x.shape
    columns = w.shape[2]
    vmem = pl.BlockSpec(memory_space=pltpu.VMEM)
    return pl.pallas_call(
        keys_queries_kernel,
        in_specs=[vmem, vmem, vmem, pl.BlockSpec(memory_space=pl.ANY), vmem, vmem],
        out_specs=[vmem, vmem, vmem],
        out_shape=[sds((rows, width), BF16)] + [sds((rows, columns), BF16)] * 2,
        scratch_shapes=[pltpu.VMEM(w.shape, BF16), pltpu.SemaphoreType.DMA((2,))],
        compiler_params=params(),
        cost_estimate=cost(4 * rows * width * columns, 4 * width * (rows + columns)),
        name="keys_queries",
    )(x, gain.reshape(1, width), bias.reshape(1, width), w, cosine, sine)


def values_kernel(normed_ref, w_ref, out_ref):
    out_ref[...] = jnp.dot(normed_ref[...], w_ref[...], preferred_element_type=F32).astype(BF16)


def project_values(normed, w, tile=256):
    rows, width = normed.shape
    columns = w.shape[1]
    return pl.pallas_call(
        values_kernel,
        grid=(columns // tile,),
        in_specs=[
            pl.BlockSpec((rows, width), lambda n: (0, 0)),
            pl.BlockSpec((width, tile), lambda n: (0, n)),
        ],
        out_specs=pl.BlockSpec((rows, tile), lambda n: (0, n)),
        out_shape=sds((rows, columns), BF16),
        compiler_params=params("arbitrary"),
        cost_estimate=cost(2 * rows * width * columns, 2 * width * (rows + columns)),
        name="project_values",
    )(normed, w)


def softmax_kernel(q_ref, k_ref, maps_ref, packet_ref):
    rows, width = q_ref.shape
    heads = width // HD
    lane = lax.broadcasted_iota(jnp.int32, (rows, HD), 1)
    table = jnp.zeros((rows, HD), F32)
    for head in range(heads):
        at = slice(head * HD, (head + 1) * HD)
        scores = lax.dot_general(
            q_ref[:, at], k_ref[:, at], (((1,), (1,)), ((), ())), preferred_element_type=F32
        ) * (1.0 / ROOT)
        top = jnp.max(scores, axis=1, keepdims=True)
        raised = jnp.exp(scores - top)
        total = jnp.sum(raised, axis=1, keepdims=True)
        maps_ref[head] = (raised * (1.0 / total)).astype(BF16)
        level = (top + jnp.log(total)) * ROOT
        high = level.astype(BF16).astype(F32)
        middle = (level - high).astype(BF16).astype(F32)
        low = (level - high - middle).astype(BF16).astype(F32)
        for piece, part in enumerate((high, middle, low)):
            table = jnp.where(lane == 3 * head + piece, part, table)
    packet_ref[0:rows, :] = q_ref[...]
    packet_ref[rows : rows + 16, :] = jnp.zeros((16, width), BF16)
    packet_ref[rows : rows + 16, 0:rows] = table.T[0:16].astype(BF16)


def softmax_maps(queries, keys):
    rows, width = queries.shape
    tokens = keys.shape[0]
    heads = width // HD
    return pl.pallas_call(
        softmax_kernel,
        out_shape=[sds((heads, rows, tokens), BF16), sds((rows + 16, width), BF16)],
        in_specs=[pl.BlockSpec(memory_space=pltpu.VMEM)] * 2,
        out_specs=[pl.BlockSpec(memory_space=pltpu.VMEM)] * 2,
        compiler_params=params(),
        cost_estimate=cost(2 * rows * tokens * width, 2 * heads * rows * tokens, heads * rows * tokens),
        name="softmax_maps",
    )(queries, keys)


def context_kernel(maps_ref, v_ref, out_ref):
    for head in range(maps_ref.shape[0]):
        at = slice(head * HD, (head + 1) * HD)
        out_ref[:, at] = jnp.dot(
            maps_ref[head], v_ref[:, at], preferred_element_type=F32
        ).astype(BF16)


def context_of(maps, values):
    heads, rows, tokens = maps.shape
    return pl.pallas_call(
        context_kernel,
        out_shape=sds((rows, heads * HD), BF16),
        in_specs=[pl.BlockSpec(memory_space=pltpu.VMEM)] * 2,
        out_specs=pl.BlockSpec(memory_space=pltpu.VMEM),
        compiler_params=params(),
        cost_estimate=cost(2 * heads * rows * tokens * HD, 2 * heads * rows * tokens),
        name="context",
    )(maps, values)


def pack_kernel(place_ref, w_ref, out_ref):
    out_ref[...] = w_ref[...]


def pack_columns(w, place, count):
    depth = w.shape[0] // 2
    tile = w.shape[1] // (2 * count)
    return pl.pallas_call(
        pack_kernel,
        grid_spec=pltpu.PrefetchScalarGridSpec(
            num_scalar_prefetch=1,
            grid=(count,),
            in_specs=[pl.BlockSpec((depth, tile), lambda n, place: (place[0], place[1 + n]))],
            out_specs=pl.BlockSpec((depth, tile), lambda n, place: (0, n)),
        ),
        out_shape=sds((depth, tile * count), BF16),
        compiler_params=params("arbitrary"),
        cost_estimate=cost(0, 4 * depth * tile * count),
        name="pack_columns",
    )(place, w)


def project_out_kernel(
    first, count, place_ref, near_ref, far_ref, w_ref, w_same_ref, w_cross_ref, *out_refs
):
    half = w_same_ref.shape[0]
    core = place_ref[0]
    same = pl.ds(pl.multiple_of(core * half, half), half)
    cross = pl.ds(pl.multiple_of((1 - core) * half, half), half)
    block = (
        jnp.dot(near_ref[...], w_ref[...], preferred_element_type=F32)
        + jnp.dot(far_ref[:, same], w_same_ref[...], preferred_element_type=F32)
        + jnp.dot(far_ref[:, cross], w_cross_ref[...], preferred_element_type=F32)
    )
    for n in range(count):

        @pl.when(pl.program_id(0) == n)
        def _(n=n):
            out_refs[n][...] = block.astype(out_refs[n].dtype)


def project_out(near, far, w, w_same, w_cross, place, first, count, dtype):
    rows, depth = near.shape
    half, wide = w_same.shape
    tile = wide // (place.shape[0] - 1)
    return pl.pallas_call(
        functools.partial(project_out_kernel, first, count),
        grid_spec=pltpu.PrefetchScalarGridSpec(
            num_scalar_prefetch=1,
            grid=(count,),
            in_specs=[
                pl.BlockSpec((rows, depth), lambda n, place: (0, 0)),
                pl.BlockSpec((rows, depth), lambda n, place: (0, 0)),
                pl.BlockSpec((depth, tile), lambda n, place: (0, place[1 + first + n])),
                pl.BlockSpec((half, tile), lambda n, place: (0, first + n)),
                pl.BlockSpec((half, tile), lambda n, place: (0, first + n)),
            ],
            out_specs=[pl.BlockSpec((rows, tile), lambda n, place: (0, 0))] * count,
        ),
        out_shape=[sds((rows, tile), dtype)] * count,
        compiler_params=params("arbitrary"),
        cost_estimate=cost(4 * rows * depth * tile * count, 2 * count * tile * (rows + 2 * depth)),
        name="project_out",
    )(place, near, far, w, w_same, w_cross)


def pair_maps_kernel(packet_ref, k_ref, own_ref, other_ref):
    rows = own_ref.shape[0]
    width = packet_ref.shape[1]
    heads = width // HD
    columns = k_ref.shape[1]
    lane_head = lax.broadcasted_iota(jnp.int32, (columns, width), 1) // HD
    wide = heads * columns
    row = lax.broadcasted_iota(jnp.int32, (16, wide), 0)
    column = lax.broadcasted_iota(jnp.int32, (16, wide), 1)
    hit = jnp.zeros((16, wide), jnp.bool_)
    for head in range(heads):
        inside = (column >= head * columns) & (column < (head + 1) * columns)
        hit = hit | (inside & (row >= 3 * head) & (row < 3 * head + 3))
    pick = jnp.where(hit, -1.0, 0.0).astype(BF16)
    level = lax.dot_general(
        packet_ref[rows : rows + 16, 0:rows],
        pick,
        (((0,), (0,)), ((), ())),
        preferred_element_type=F32,
    )
    for place, out_ref in enumerate((own_ref, other_ref)):
        k = k_ref[place].astype(F32)
        spread = jnp.concatenate(
            [jnp.where(lane_head == head, k, 0.0) for head in range(heads)], axis=0
        ).astype(BF16)
        scores = lax.dot_general(
            packet_ref[0:rows, :], spread, (((1,), (1,)), ((), ())), preferred_element_type=F32
        )
        out_ref[...] = jnp.exp((scores + level) * (1.0 / ROOT)).astype(BF16)


def pair_maps(packet, keys):
    rows, width = packet.shape[0] - 16, packet.shape[1]
    wide = (width // HD) * keys.shape[1]
    return pl.pallas_call(
        pair_maps_kernel,
        out_shape=[sds((rows, wide), BF16)] * 2,
        in_specs=[pl.BlockSpec(memory_space=pltpu.VMEM)] * 2,
        out_specs=[pl.BlockSpec(memory_space=pltpu.VMEM)] * 2,
        compiler_params=params(),
        cost_estimate=cost(4 * rows * wide * width, 8 * rows * wide, 2 * rows * wide),
        name="pair_maps",
    )(packet, keys)


def pair_kernel(factor, count, chained, *refs):
    maps_refs = refs[:count]
    (w_maps_ref, b_maps_ref, gain_ref, bias_ref, w_up_ref, b_up_ref, w_down_ref, b_down_ref) = refs[
        count : count + 8
    ]
    out_ref, spread_ref, up_ref, shift_ref, rows_ref = refs[count + 8 + chained :]
    block = out_ref.shape[0]
    columns = out_ref.shape[1]
    chunk = 8 * columns
    channels = out_ref.shape[2]
    heads_all = w_maps_ref.shape[0]
    heads = heads_all // count
    group = HD // heads_all

    @pl.when(pl.program_id(0) == 0)
    def _():
        w = w_maps_ref[...].astype(F32)
        w = (w - jnp.sum(w, axis=1, keepdims=True) * (1.0 / channels)) * factor
        high = w.astype(BF16)
        low = (w - high.astype(F32)).astype(BF16)
        spread_ref[...] = jnp.zeros_like(spread_ref)
        for i in range(group):
            at = slice(i * channels, (i + 1) * channels)
            spread_ref[i * heads_all : (i + 1) * heads_all, at] = high
            spread_ref[HD + i * heads_all : HD + (i + 1) * heads_all, at] = low
        b = b_maps_ref[...]
        b = b - jnp.sum(b, axis=1, keepdims=True) * (1.0 / channels)
        shift_ref[...] = jnp.concatenate([b] * group, axis=1)
        up_ref[0:channels, :] = w_up_ref[...]
        b_up = b_up_ref[...]
        top = b_up.astype(BF16).astype(F32)
        middle = (b_up - top).astype(BF16).astype(F32)
        tail = jnp.concatenate(
            [top, middle, b_up - top - middle, jnp.zeros((channels - 3, b_up.shape[1]), F32)], axis=0
        )
        up_ref[channels : 2 * channels, :] = tail.astype(BF16)
        rows_ref[...] = jnp.zeros_like(rows_ref)

    def fill():
        for source in range(count):
            wide = maps_refs[source][...].astype(F32)
            for head in range(heads):
                place = (source * heads + head) * block
                rows_ref[place : place + block, 0:columns] = wide[
                    :, head * columns : (head + 1) * columns
                ]

    gain, bias = gain_ref[...], bias_ref[...]

    def normalise(g):
        tall = jnp.concatenate(
            [rows_ref[pl.ds(g * group + i, heads_all, stride=block), :] for i in range(group)], axis=0
        )
        flat = tall.T[0:columns].astype(BF16)
        mixed = (
            jnp.dot(
                jnp.concatenate([flat, flat], axis=1), spread_ref[...], preferred_element_type=F32
            )
            + shift_ref[...]
        )
        pieces = []
        for i in range(group):
            centered = mixed[:, i * channels : (i + 1) * channels]
            variance = jnp.sum(centered * centered, axis=1, keepdims=True) * (1.0 / channels)
            pieces.append((centered * lax.rsqrt(variance + 1e-05) * gain + bias).astype(BF16))
        return jnp.concatenate(pieces, axis=0)

    lane = lax.broadcasted_iota(jnp.int32, (chunk, channels), 1)
    unit = jnp.where(lane < 3, 1.0, 0.0).astype(BF16)

    def transition(normed, at):
        hidden = jnp.dot(
            jnp.concatenate([normed, unit], axis=1), up_ref[...], preferred_element_type=F32
        )
        hidden = jnp.maximum(hidden, 0.0).astype(BF16)
        result = jnp.dot(hidden, w_down_ref[...], preferred_element_type=F32) + b_down_ref[...]
        result = result.astype(BF16)
        for i in range(chunk // columns):
            out_ref[at + i] = result[i * columns : (i + 1) * columns]

    fill()
    per = chunk // columns // group
    waiting = None
    for first in range(0, block // group, per):
        normed = jnp.concatenate([normalise(g) for g in range(first, first + per)], axis=0)
        if waiting is not None:
            transition(*waiting)
        waiting = (normed, first * group)
    transition(*waiting)


def pair_block_fast(
    maps,
    w_maps,
    b_maps,
    pair_gain,
    pair_bias,
    w_up,
    b_up,
    w_down,
    b_down,
    factor,
    columns,
    block=64,
    first=0,
    blocks=None,
    begun=None,
):
    count = len(maps)
    rows, wide = maps[0].shape
    channels, hidden = w_up.shape
    heads_all = w_maps.shape[0]
    group = HD // heads_all
    whole = lambda *shape: pl.BlockSpec(shape, lambda n: (0,) * len(shape))
    blocks = rows // block if blocks is None else blocks
    pairs = blocks * block * columns
    chained = [] if begun is None else [begun]
    return pl.pallas_call(
        functools.partial(pair_kernel, factor, count, len(chained)),
        grid=(blocks,),
        in_specs=[pl.BlockSpec((block, wide), lambda n: (first + n, 0))] * count
        + [
            whole(heads_all, channels),
            whole(1, channels),
            whole(1, channels),
            whole(1, channels),
            whole(channels, hidden),
            whole(1, hidden),
            whole(hidden, channels),
            whole(1, channels),
        ]
        + [pl.BlockSpec(memory_space=pl.ANY)] * len(chained),
        out_specs=pl.BlockSpec((block, columns, channels), lambda n: (first + n, 0, 0)),
        out_shape=sds((rows, columns, channels), BF16),
        scratch_shapes=[
            pltpu.VMEM((2 * HD, group * channels), BF16),
            pltpu.VMEM((2 * channels, hidden), BF16),
            pltpu.VMEM((1, group * channels), F32),
            pltpu.VMEM((heads_all * block, HD), F32),
        ],
        input_output_aliases={count + 8: 0} if chained else {},
        compiler_params=params("arbitrary"),
        cost_estimate=cost(4 * pairs * channels * hidden, 4 * pairs * channels, pairs * channels),
        name="pair_block",
    )(
        *maps,
        w_maps,
        b_maps.reshape(1, -1),
        pair_gain.reshape(1, -1),
        pair_bias.reshape(1, -1),
        w_up,
        b_up.reshape(1, -1),
        w_down,
        b_down.reshape(1, -1),
        *chained,
    )


def per_device_fast(
    layer_input,
    norm_gain,
    norm_bias,
    w_query_key,
    w_value,
    w_out,
    w_maps,
    b_maps,
    pair_gain,
    pair_bias,
    w_up,
    b_up,
    w_down,
    b_down,
):
    rows = layer_input.shape[0]
    parts = lax.axis_size("mp")
    ring = parts // 2
    tokens = rows * lax.axis_size("rows")
    columns = tokens // parts
    heads = w_value.shape[1] // HD
    core = lax.axis_index("rows")
    z, y = lax.axis_index("mp") // 2, lax.axis_index("mp") % 2

    swap_core = [(0, 1), (1, 0)]
    swap_y = [(m, m ^ 1) for m in range(parts)]

    def rotate_z(by):
        return [(2 * a + b, 2 * ((a + by) % ring) + b) for a in range(ring) for b in range(2)]

    half = HD // 2
    freqs = 10000.0 ** (-jnp.arange(half, dtype=F32) / half)
    positions = core * rows + jnp.arange(rows, dtype=jnp.int32)
    angles = positions.astype(F32)[:, None] * freqs[None, :]
    cosine, sine = jnp.cos(angles), jnp.sin(angles)
    cosine = jnp.concatenate([cosine, cosine], axis=1)
    sine = jnp.concatenate([-sine, sine], axis=1)

    ahead = (z - 1 - jnp.arange(ring, dtype=jnp.int32)) % ring
    core_at = core.astype(jnp.int32)[None]
    w_sent = pack_columns(w_out, jnp.concatenate([core_at, 2 * ahead + 1 - y]), ring)
    w_same = lax.ppermute(w_sent, "mp", swap_y)

    normed, keys, queries = keys_queries(
        layer_input, norm_gain, norm_bias, w_query_key, cosine, sine
    )
    keys_there = lax.ppermute(keys, "rows", swap_core)
    values = project_values(normed, w_value)
    first = core == 0
    keys_all = jnp.concatenate(
        [jnp.where(first, keys, keys_there), jnp.where(first, keys_there, keys)], axis=0
    )
    values_there = lax.ppermute(values, "rows", swap_core)
    maps, packet = softmax_maps(queries, keys_all)
    packets = [packet]
    packets.append(lax.ppermute(packet, "mp", rotate_z(1)))

    chips = keys_all.reshape(ring, 2, columns, -1)
    shares = lax.dynamic_index_in_dim(chips, core, axis=1, keepdims=False)
    mine = jnp.stack(
        [
            lax.ppermute(
                lax.dynamic_index_in_dim(shares, (z + d) % ring, 0, keepdims=False),
                "mp",
                rotate_z(d),
            )
            for d in range(1, ring)
        ]
    )
    theirs = lax.ppermute(mine, "rows", swap_core)
    here = y == core
    key_columns = jnp.stack([jnp.where(here, mine, theirs), jnp.where(here, theirs, mine)], axis=1)
    local = lax.dynamic_index_in_dim(chips, z, 0, keepdims=False)
    local = jnp.where(y == 0, local, local[::-1])

    values_all = jnp.concatenate(
        [jnp.where(first, values, values_there), jnp.where(first, values_there, values)], axis=0
    )
    near = context_of(maps, values_all)
    far = lax.ppermute(near, "mp", swap_y)
    w_cross = lax.ppermute(w_same, "rows", swap_core)

    own_maps, other_maps = [], []
    for d in range(ring):
        if d >= 2:
            packets.append(lax.ppermute(packets[-1], "mp", rotate_z(1)))
        own, other = pair_maps(packets[d], local if d == 0 else key_columns[d - 1])
        own_maps.append(own)
        other_maps.append(lax.ppermute(other, "mp", swap_y))

    place = jnp.concatenate([core_at, 2 * ahead + y])
    out = functools.partial(project_out, near, far, w_out, w_same, w_cross, place)
    (head,) = out(0, 1, BF16)
    tails = out(1, ring - 1, F32)

    source = (z - jnp.arange(ring, dtype=jnp.int32)) % ring
    head_order = jnp.concatenate([2 * source + y, 2 * source + 1 - y])
    w_sorted = w_maps.reshape(parts, heads, -1)[head_order].reshape(w_maps.shape)
    pair = functools.partial(
        pair_block_fast,
        own_maps + other_maps,
        w_sorted,
        b_maps,
        pair_gain,
        pair_bias,
        w_up,
        b_up,
        w_down,
        b_down,
        float(tokens),
        columns,
    )
    pair_features = None
    blocks = rows // 48
    for n, tail in enumerate(tails):
        running = lax.ppermute(head, "mp", rotate_z(1))
        pair_features = pair(
            block=48, first=n * blocks // 4, blocks=blocks // 4, begun=pair_features
        )
        total = tail + running.astype(F32)
        head = total.astype(BF16)
    attention = total
    pair_features = pair(block=48, first=3 * blocks // 4, blocks=blocks // 4, begun=pair_features)
    return (attention, pair_features)


def layer_norm(values, gain, bias):
    average = jnp.mean(values, axis=-1, keepdims=True)
    centered = values - average
    variance = jnp.mean(centered * centered, axis=-1, keepdims=True)
    return centered * lax.rsqrt(variance + 1e-05) * gain + bias


def rotate(values, positions):
    half = values.shape[-1] // 2
    freqs = 10000.0 ** (-jnp.arange(half, dtype=jnp.float32) / half)
    angles = positions.astype(jnp.float32)[:, None] * freqs[None, :]
    cosine = jnp.cos(angles)[:, None, :]
    sine = jnp.sin(angles)[:, None, :]
    lower = values[..., :half]
    upper = values[..., half:]
    return jnp.concatenate([lower * cosine - upper * sine, upper * cosine + lower * sine], axis=-1)


def project_rotated(normed, weight, positions):
    count = normed.shape[0]
    projected = jnp.dot(normed, weight, preferred_element_type=jnp.float32)
    projected = projected.reshape(count, weight.shape[1] // HD, HD)
    return rotate(projected, positions).astype(jnp.bfloat16).reshape(count, weight.shape[1])


def pair_block(maps, w_maps, b_maps, pair_gain, pair_bias, w_up, b_up, w_down, b_down, factor):
    mixed = (
        jnp.einsum("hrc,hp->rcp", maps, w_maps, preferred_element_type=jnp.float32) * factor
        + b_maps
    )
    normed = layer_norm(mixed, pair_gain, pair_bias).astype(jnp.bfloat16)
    hidden = jax.nn.relu(
        jnp.einsum("rcp,pt->rct", normed, w_up, preferred_element_type=jnp.float32) + b_up
    ).astype(jnp.bfloat16)
    return (
        jnp.einsum("rct,tp->rcp", hidden, w_down, preferred_element_type=jnp.float32) + b_down
    ).astype(jnp.bfloat16)


def per_device(
    layer_input,
    norm_gain,
    norm_bias,
    w_query_key,
    w_value,
    w_out,
    w_maps,
    b_maps,
    pair_gain,
    pair_bias,
    w_up,
    b_up,
    w_down,
    b_down,
):
    tok_rows = layer_input.shape[0]
    tokens_all = tok_rows * lax.axis_size("rows")
    local_heads = w_value.shape[1] // HD
    normed = layer_norm(layer_input.astype(jnp.float32), norm_gain, norm_bias).astype(jnp.bfloat16)
    own_positions = lax.axis_index("rows") * tok_rows + jnp.arange(tok_rows, dtype=jnp.int32)
    queries = project_rotated(normed, w_query_key[0], own_positions)
    keys_local = project_rotated(normed, w_query_key[1], own_positions)
    values_local = jnp.dot(normed, w_value, preferred_element_type=jnp.float32).astype(jnp.bfloat16)
    keys_all, values_all = (
        lax.all_gather(keys_local, "rows", axis=0, tiled=True),
        lax.all_gather(values_local, "rows", axis=0, tiled=True),
    )
    head_queries = queries.reshape(tok_rows, local_heads, HD)
    head_keys = keys_all.reshape(tokens_all, local_heads, HD)
    head_values = values_all.reshape(tokens_all, local_heads, HD)
    scores = jnp.einsum(
        "qhd,khd->hqk", head_queries, head_keys, preferred_element_type=jnp.float32
    ) / math.sqrt(HD)
    maps = jax.nn.softmax(scores, axis=-1).astype(jnp.bfloat16)
    context = jnp.einsum("hqk,khd->qhd", maps, head_values, preferred_element_type=jnp.float32)
    context = context.astype(jnp.bfloat16).reshape(tok_rows, local_heads * HD)
    partial_sums = jnp.dot(context, w_out, preferred_element_type=jnp.float32)
    attention = lax.psum_scatter(partial_sums, "mp", scatter_dimension=1, tiled=True)
    factor = float(tokens_all)
    pair_features = pair_block(
        lax.all_to_all(maps, "mp", split_axis=2, concat_axis=0, tiled=True),
        w_maps,
        b_maps,
        pair_gain,
        pair_bias,
        w_up,
        b_up,
        w_down,
        b_down,
        factor,
    )
    return (attention, pair_features)


def solution(mesh):
    in_specs = (
        P(("groups", "rows"), None),
        P(),
        P(),
        P(None, None, "mp"),
        P(None, "mp"),
        P("mp", None),
        P(),
        P(),
        P(),
        P(),
        P(),
        P(),
        P(),
        P(),
    )
    out_specs = (P(("groups", "rows"), "mp"), P(("groups", "rows"), "mp", None))
    small = mesh.shape["mp"] == 8 and mesh.shape["rows"] == 2
    return jax.shard_map(
        per_device_fast if small else per_device, mesh=mesh, in_specs=in_specs, out_specs=out_specs, check_vma=False
    )
```

```python
import functools
import math

import jax
import jax.numpy as jnp
from jax import lax
from jax.experimental import pallas as pl
from jax.experimental.pallas import tpu as pltpu
from jax.sharding import PartitionSpec as P


HD = 128
F32 = jnp.float32
BF16 = jnp.bfloat16
ROOT = math.sqrt(HD)


def params(*axes, mib=24):
    return pltpu.CompilerParams(
        dimension_semantics=axes if axes else None, vmem_limit_bytes=mib * 1024 * 1024
    )


def cost(flops, moved, transcendentals=0):
    return pl.CostEstimate(
        flops=int(flops), bytes_accessed=int(moved), transcendentals=int(transcendentals)
    )


def sds(shape, dtype):
    return jax.ShapeDtypeStruct(shape, dtype)


VMEM = pl.BlockSpec(memory_space=pltpu.VMEM)
ANYWHERE = pl.BlockSpec(memory_space=pl.ANY)
HBM = pl.BlockSpec(memory_space=pltpu.HBM)
SMEM = pl.BlockSpec(memory_space=pltpu.SMEM)


def turn(block, cosine, sine):
    pieces = []
    for head in range(block.shape[1] // HD):
        one = block[:, head * HD : (head + 1) * HD]
        pieces.append(one * cosine + pltpu.roll(one, HD // 2, 1) * sine)
    return jnp.concatenate(pieces, axis=1)


def project_kernel(
    x_ref, gain_ref, bias_ref, wqk_ref, wv_ref, cos_ref, sin_ref, q_ref, kv_ref, x, normed, w, x_sems, w_sems
):
    rows, width = x.shape
    columns = q_ref.shape[1]
    step, chunks, tile = 16, x_sems.shape[0], min(256, columns)
    parts = w_sems.shape[1]
    deep = width // parts
    piece = rows // chunks
    x_copies = [
        pltpu.make_async_copy(
            x_ref.at[n * piece : (n + 1) * piece], x.at[n * piece : (n + 1) * piece], x_sems.at[n]
        )
        for n in range(chunks)
    ]
    sources = (wqk_ref.at[1], wqk_ref.at[0], wv_ref)
    w_copies = [
        pltpu.make_async_copy(
            source.at[n * deep : (n + 1) * deep],
            w.at[which, n * deep : (n + 1) * deep],
            w_sems.at[which, n],
        )
        for which, source in enumerate(sources)
        for n in range(parts)
    ]
    for copy in x_copies + w_copies:
        copy.start()

    def body(i, carry):
        at = pl.ds(pl.multiple_of(i * step, step), step)

        def lanes(n):
            return slice(n * HD, (n + 1) * HD)

        def total(one):
            parts = [jnp.zeros((step, HD), F32) for _ in range(4)]
            for n in range(width // HD):
                parts[n % 4] = parts[n % 4] + one(x[at, lanes(n)].astype(F32))
            whole = (parts[0] + parts[1]) + (parts[2] + parts[3])
            return jnp.sum(whole, axis=1, keepdims=True) * (1.0 / width)

        mean = total(lambda v: v)
        variance = total(lambda v: (v - mean) * (v - mean))
        scale = lax.rsqrt(variance + 1e-05)
        for n in range(width // HD):
            scaled = (x[at, lanes(n)].astype(F32) - mean) * scale
            normed[at, lanes(n)] = (scaled * gain_ref[:, lanes(n)] + bias_ref[:, lanes(n)]).astype(BF16)
        return carry

    for n in range(chunks):
        x_copies[n].wait()
        lax.fori_loop(n * piece // step, (n + 1) * piece // step, body, 0, unroll=2)
    cosine = jnp.concatenate([cos_ref[...], cos_ref[...]], axis=1)
    sine = jnp.concatenate([-sin_ref[...], sin_ref[...]], axis=1)
    for which in range(3):
        for n in range(parts):
            w_copies[which * parts + n].wait()
        for n in range(columns // tile):
            block = jnp.dot(
                normed[...], w[which, :, n * tile : (n + 1) * tile], preferred_element_type=F32
            )
            if which < 2:
                block = turn(block, cosine, sine)
            at = n * tile
            if which == 0:
                kv_ref[:, at : at + tile] = block.astype(BF16)
            elif which == 1:
                q_ref[:, at : at + tile] = block.astype(BF16)
            else:
                kv_ref[:, columns + at : columns + at + tile] = block.astype(BF16)


def project(x, gain, bias, w_query_key, w_value, cosine, sine):
    rows, width = x.shape
    columns = w_value.shape[1]
    return pl.pallas_call(
        project_kernel,
        in_specs=[HBM, VMEM, VMEM, HBM, HBM, VMEM, VMEM],
        out_specs=[VMEM, VMEM],
        out_shape=[sds((rows, columns), BF16), sds((rows, 2 * columns), BF16)],
        scratch_shapes=[
            pltpu.VMEM((rows, width), BF16),
            pltpu.VMEM((rows, width), BF16),
            pltpu.VMEM((3, width, columns), BF16),
            pltpu.SemaphoreType.DMA((4,)),
            pltpu.SemaphoreType.DMA((3, 2)),
        ],
        compiler_params=params(mib=44),
        cost_estimate=cost(6 * rows * width * columns, 2 * width * (rows + 3 * columns)),
        name="project",
    )(x, gain.reshape(1, width), bias.reshape(1, width), w_query_key, w_value, cosine, sine)


def attend_kernel(
    ring, at_ref, q_ref, own_ref, there_ref, context_ref, local_ref, *rest
):
    share_refs, level_ref = rest[:-1], rest[-1]
    rows, width = q_ref.shape
    heads = width // HD
    columns = local_ref.shape[0] // 2 - 8
    core, z, y = at_ref[0], at_ref[1], at_ref[2]
    lane = lax.broadcasted_iota(jnp.int32, (rows, HD), 1)
    table = jnp.zeros((rows, HD), F32)
    contract = (((1,), (1,)), ((), ()))
    for head in range(heads):
        at = slice(head * HD, (head + 1) * HD)
        at_v = slice(width + head * HD, width + (head + 1) * HD)
        scores = [
            lax.dot_general(q_ref[:, at], ref[:, at], contract, preferred_element_type=F32)
            * (1.0 / ROOT)
            for ref in (own_ref, there_ref)
        ]
        top = jnp.max(jnp.maximum(scores[0], scores[1]), axis=1, keepdims=True)
        raised = [jnp.exp(part - top) for part in scores]
        total = jnp.sum(raised[0] + raised[1], axis=1, keepdims=True)
        inverse = 1.0 / total
        maps = [(part * inverse).astype(BF16) for part in raised]
        context_ref[:, at] = (
            jnp.dot(maps[0], own_ref[:, at_v], preferred_element_type=F32)
            + jnp.dot(maps[1], there_ref[:, at_v], preferred_element_type=F32)
        ).astype(BF16)
        level = (top + jnp.log(total)) * ROOT
        high = level.astype(BF16).astype(F32)
        middle = (level - high).astype(BF16).astype(F32)
        low = (level - high - middle).astype(BF16).astype(F32)
        for piece, part in enumerate((high, middle, low)):
            table = jnp.where(lane == 3 * head + piece, part, table)
    level_ref[...] = jnp.zeros_like(level_ref)
    level_ref[:, 0:rows] = table.T[0:16].astype(BF16)

    def key_rows(chip, which):
        token = chip * (2 * columns) + which * columns
        holder = (token >= rows).astype(jnp.int32)
        start = pl.ds(pl.multiple_of(token - holder * rows, 32), columns)
        mine = (holder == core).astype(F32)
        near = own_ref[start, 0:width].astype(F32)
        far = there_ref[start, 0:width].astype(F32)
        return (near * mine + far * (1.0 - mine)).astype(BF16)

    local_ref[0:columns, :] = key_rows(z, y)
    local_ref[columns : 2 * columns, :] = key_rows(z, 1 - y)
    local_ref[2 * columns : 2 * columns + 16, :] = level_ref[...]
    for distance, share_ref in enumerate(share_refs, 1):
        chip = lax.rem(z + distance, ring)
        share_ref[0:columns, :] = key_rows(chip, core)
        share_ref[columns : columns + 16, :] = level_ref[...]


def attend(at, queries, own, there, ring, columns):
    rows, width = queries.shape
    tokens = 2 * rows
    return pl.pallas_call(
        functools.partial(attend_kernel, ring),
        in_specs=[SMEM, VMEM, VMEM, VMEM],
        out_specs=[VMEM] * (ring + 1),
        out_shape=[sds((rows, width), BF16), sds((2 * columns + 16, width), BF16)]
        + [sds((columns + 16, width), BF16)] * (ring - 1),
        scratch_shapes=[pltpu.VMEM((16, width), BF16)],
        compiler_params=params(),
        cost_estimate=cost(4 * rows * tokens * width, 8 * rows * width, rows * tokens * width // HD),
        name="attend",
    )(at, queries, own, there)


def pack_kernel(count, at_ref, w_ref, out_ref, sems):
    depth, wide = out_ref.shape
    tile = wide // count
    core, z, y = at_ref[0], at_ref[1], at_ref[2]
    copies = []
    for n in range(count):
        block = 2 * lax.rem(z + (2 * count - 1 - n), count) + 1 - y
        copies.append(
            pltpu.make_async_copy(
                w_ref.at[
                    pl.ds(pl.multiple_of(core * depth, depth), depth),
                    pl.ds(pl.multiple_of(block * tile, tile), tile),
                ],
                out_ref.at[:, n * tile : (n + 1) * tile],
                sems.at[n],
            )
        )
    for copy in copies:
        copy.start()
    for copy in copies:
        copy.wait()


def pack_columns(at, w, count):
    depth, wide = w.shape[0] // 2, w.shape[1] // 2
    return pl.pallas_call(
        functools.partial(pack_kernel, count),
        in_specs=[SMEM, HBM],
        out_specs=VMEM,
        out_shape=sds((depth, wide), BF16),
        scratch_shapes=[pltpu.SemaphoreType.DMA((count,))],
        compiler_params=params(),
        cost_estimate=cost(0, 4 * depth * wide),
        name="pack_columns",
    )(at, w)


def project_out_kernel(at_ref, near_ref, far_ref, w_ref, w_same_ref, w_cross_ref, *rest):
    out_refs, (w, sems) = rest[:-2], rest[-2:]
    count = len(out_refs)
    tile = out_refs[0].shape[1]
    half = w_same_ref.shape[0]
    core, z, y = at_ref[0], at_ref[1], at_ref[2]
    copies = []
    for n in range(count):
        block = 2 * lax.rem(z + (2 * count - 1 - n), count) + y
        copies.append(
            pltpu.make_async_copy(
                w_ref.at[:, pl.ds(pl.multiple_of(block * tile, tile), tile)], w.at[n], sems.at[n]
            )
        )
    for copy in copies:
        copy.start()
    same = far_ref[:, pl.ds(pl.multiple_of(core * half, half), half)]
    cross = far_ref[:, pl.ds(pl.multiple_of((1 - core) * half, half), half)]
    for n, out_ref in enumerate(out_refs):
        lanes = slice(n * tile, (n + 1) * tile)
        block = jnp.dot(same, w_same_ref[:, lanes], preferred_element_type=F32) + jnp.dot(
            cross, w_cross_ref[:, lanes], preferred_element_type=F32
        )
        copies[n].wait()
        block = block + jnp.dot(near_ref[...], w[n], preferred_element_type=F32)
        out_ref[...] = block.astype(out_ref.dtype)


def project_out(at, near, far, w, w_same, w_cross, count):
    rows, depth = near.shape
    _, wide = w_same.shape
    tile = wide // count
    return pl.pallas_call(
        project_out_kernel,
        in_specs=[SMEM, VMEM, VMEM, ANYWHERE, VMEM, VMEM],
        out_specs=[VMEM] * count,
        out_shape=[sds((rows, tile), BF16)] + [sds((rows, tile), F32)] * (count - 1),
        scratch_shapes=[
            pltpu.VMEM((count, depth, tile), BF16),
            pltpu.SemaphoreType.DMA((count,)),
        ],
        compiler_params=params(),
        cost_estimate=cost(4 * rows * depth * wide, 4 * wide * (rows + depth)),
        name="project_out",
    )(at, near, far, w, w_same, w_cross)


def pair_maps_kernel(sources, at_ref, *refs):
    own_ref, other_ref = refs[-2:]
    rows = own_ref.shape[1]
    width = refs[0].shape[1]
    heads = width // HD
    wide = own_ref.shape[2]
    columns = wide // heads
    lane_head = lax.broadcasted_iota(jnp.int32, (columns, width), 1) // HD
    row = lax.broadcasted_iota(jnp.int32, (16, wide), 0)
    column = lax.broadcasted_iota(jnp.int32, (16, wide), 1)
    hit = jnp.zeros((16, wide), jnp.bool_)
    for head in range(heads):
        inside = (column >= head * columns) & (column < (head + 1) * columns)
        hit = hit | (inside & (row >= 3 * head) & (row < 3 * head + 3))
    pick = jnp.where(hit, -1.0, 0.0).astype(BF16)
    straight = (at_ref[2] == at_ref[0]).astype(F32)
    taken = 0
    for place, count in enumerate(sources):
        q_ref, keys = refs[taken], refs[taken + 1 : taken + count]
        taken += count
        if count == 2:
            pieces = [keys[0][n * columns : (n + 1) * columns, :].astype(F32) for n in range(2)]
            levels = keys[0][2 * columns : 2 * columns + 16, 0:rows]
        else:
            mine = keys[0][0:columns, :].astype(F32)
            theirs = keys[1][0:columns, :].astype(F32)
            pieces = [
                mine * straight + theirs * (1.0 - straight),
                theirs * straight + mine * (1.0 - straight),
            ]
            levels = keys[0][columns : columns + 16, 0:rows]
        level = lax.dot_general(
            levels, pick, (((0,), (0,)), ((), ())), preferred_element_type=F32
        )
        for k, out_ref in zip(pieces, (own_ref, other_ref)):
            spread = jnp.concatenate(
                [jnp.where(lane_head == head, k, 0.0).astype(BF16) for head in range(heads)], axis=0
            )
            scores = lax.dot_general(
                q_ref[...], spread, (((1,), (1,)), ((), ())), preferred_element_type=F32
            )
            out_ref[place] = jnp.exp((scores + level) * (1.0 / ROOT)).astype(BF16)


def pair_maps(at, sources, columns):
    rows, width = sources[0][0].shape
    wide = (width // HD) * columns
    count = len(sources)
    flat = [array for source in sources for array in source]
    return pl.pallas_call(
        functools.partial(pair_maps_kernel, [len(source) for source in sources]),
        in_specs=[SMEM] + [VMEM] * len(flat),
        out_specs=[VMEM] * 2,
        out_shape=[sds((count, rows, wide), BF16)] * 2,
        compiler_params=params(),
        cost_estimate=cost(
            4 * count * rows * wide * width, 8 * count * rows * wide, 2 * count * rows * wide
        ),
        name="pair_maps",
    )(at, *flat)


def pair_kernel(factor, inputs, count, chained, at_ref, *refs):
    maps_refs = refs[:inputs]
    (w_maps_ref, b_maps_ref, gain_ref, bias_ref, w_up_ref, b_up_ref, w_down_ref, b_down_ref) = refs[
        inputs : inputs + 8
    ]
    out_ref, spread_ref, up_ref, shift_ref, rows_ref = refs[inputs + 8 + chained :]
    block = out_ref.shape[0]
    columns = out_ref.shape[1]
    chunk = 8 * columns
    channels = out_ref.shape[2]
    heads_all = w_maps_ref.shape[0]
    heads = heads_all // count
    group = HD // heads_all

    @pl.when(pl.program_id(0) == 0)
    def _():
        row = lax.broadcasted_iota(jnp.int32, (heads_all, heads_all), 0)
        column = lax.broadcasted_iota(jnp.int32, (heads_all, heads_all), 1)
        ring = count // 2
        distance = lax.rem(row // heads, ring)
        chip = lax.rem(at_ref[1] + ring - distance, ring)
        side = jnp.where(row // heads >= ring, 1 - at_ref[2], at_ref[2])
        head = (2 * chip + side) * heads + lax.rem(row, heads)
        sort = jnp.where(column == head, 1.0, 0.0).astype(BF16)
        w = jnp.dot(sort, w_maps_ref[...], preferred_element_type=F32)
        w = (w - jnp.sum(w, axis=1, keepdims=True) * (1.0 / channels)) * factor
        high = w.astype(BF16)
        low = (w - high.astype(F32)).astype(BF16)
        spread_ref[...] = jnp.zeros_like(spread_ref)
        for i in range(group):
            at = slice(i * channels, (i + 1) * channels)
            spread_ref[i * heads_all : (i + 1) * heads_all, at] = high
            spread_ref[HD + i * heads_all : HD + (i + 1) * heads_all, at] = low
        b = b_maps_ref[...]
        b = b - jnp.sum(b, axis=1, keepdims=True) * (1.0 / channels)
        shift_ref[...] = jnp.concatenate([b] * group, axis=1)
        up_ref[0:channels, :] = w_up_ref[...]
        b_up = b_up_ref[...]
        top = b_up.astype(BF16).astype(F32)
        middle = (b_up - top).astype(BF16).astype(F32)
        tail = jnp.concatenate(
            [top, middle, b_up - top - middle, jnp.zeros((channels - 3, b_up.shape[1]), F32)], axis=0
        )
        up_ref[channels : 2 * channels, :] = tail.astype(BF16)
        rows_ref[...] = jnp.zeros_like(rows_ref)

    def fill():
        lots = [(ref, n) for ref in maps_refs for n in range(ref.shape[0])]
        for source, (ref, n) in enumerate(lots):
            wide = ref[n].astype(F32)
            for head in range(heads):
                place = (source * heads + head) * block
                rows_ref[place : place + block, 0:columns] = wide[
                    :, head * columns : (head + 1) * columns
                ]

    gain, bias = gain_ref[...], bias_ref[...]

    def normalise(g):
        tall = jnp.concatenate(
            [rows_ref[pl.ds(g * group + i, heads_all, stride=block), :] for i in range(group)], axis=0
        )
        flat = tall.T[0:columns].astype(BF16)
        mixed = (
            jnp.dot(
                jnp.concatenate([flat, flat], axis=1), spread_ref[...], preferred_element_type=F32
            )
            + shift_ref[...]
        )
        pieces = []
        for i in range(group):
            centered = mixed[:, i * channels : (i + 1) * channels]
            variance = jnp.sum(centered * centered, axis=1, keepdims=True) * (1.0 / channels)
            pieces.append((centered * lax.rsqrt(variance + 1e-05) * gain + bias).astype(BF16))
        return jnp.concatenate(pieces, axis=0)

    lane = lax.broadcasted_iota(jnp.int32, (chunk, channels), 1)
    unit = jnp.where(lane < 3, 1.0, 0.0).astype(BF16)

    def transition(normed, at):
        hidden = jnp.dot(
            jnp.concatenate([normed, unit], axis=1), up_ref[...], preferred_element_type=F32
        )
        hidden = jnp.maximum(hidden, 0.0).astype(BF16)
        result = jnp.dot(hidden, w_down_ref[...], preferred_element_type=F32) + b_down_ref[...]
        result = result.astype(BF16)
        for i in range(chunk // columns):
            out_ref[at + i] = result[i * columns : (i + 1) * columns]

    fill()
    per = chunk // columns // group
    waiting = None
    for first in range(0, block // group, per):
        normed = jnp.concatenate([normalise(g) for g in range(first, first + per)], axis=0)
        if waiting is not None:
            transition(*waiting)
        waiting = (normed, first * group)
    transition(*waiting)


def pair_block_fast(
    at,
    maps,
    w_maps,
    b_maps,
    pair_gain,
    pair_bias,
    w_up,
    b_up,
    w_down,
    b_down,
    factor,
    columns,
    block=64,
    first=0,
    blocks=None,
    begun=None,
):
    count = sum(array.shape[0] for array in maps)
    rows, wide = maps[0].shape[1:]
    channels, hidden = w_up.shape
    heads_all = w_maps.shape[0]
    group = HD // heads_all
    whole = lambda *shape: pl.BlockSpec(shape, lambda n: (0,) * len(shape))
    blocks = rows // block if blocks is None else blocks
    pairs = blocks * block * columns
    chained = [] if begun is None else [begun]
    return pl.pallas_call(
        functools.partial(pair_kernel, factor, len(maps), count, len(chained)),
        grid=(blocks,),
        in_specs=[SMEM]
        + [
            pl.BlockSpec((array.shape[0], block, wide), lambda n: (0, first + n, 0))
            for array in maps
        ]
        + [
            whole(heads_all, channels),
            whole(1, channels),
            whole(1, channels),
            whole(1, channels),
            whole(channels, hidden),
            whole(1, hidden),
            whole(hidden, channels),
            whole(1, channels),
        ]
        + [pl.BlockSpec(memory_space=pl.ANY)] * len(chained),
        out_specs=pl.BlockSpec((block, columns, channels), lambda n: (first + n, 0, 0)),
        out_shape=sds((rows, columns, channels), BF16),
        scratch_shapes=[
            pltpu.VMEM((2 * HD, group * channels), BF16),
            pltpu.VMEM((2 * channels, hidden), BF16),
            pltpu.VMEM((1, group * channels), F32),
            pltpu.VMEM((heads_all * block, HD), F32),
        ],
        input_output_aliases={len(maps) + 9: 0} if chained else {},
        compiler_params=params("arbitrary"),
        cost_estimate=cost(4 * pairs * channels * hidden, 4 * pairs * channels, pairs * channels),
        name="pair_block",
    )(
        at,
        *maps,
        w_maps,
        b_maps.reshape(1, -1),
        pair_gain.reshape(1, -1),
        pair_bias.reshape(1, -1),
        w_up,
        b_up.reshape(1, -1),
        w_down,
        b_down.reshape(1, -1),
        *chained,
    )


def per_device_fast(
    layer_input,
    norm_gain,
    norm_bias,
    w_query_key,
    w_value,
    w_out,
    w_maps,
    b_maps,
    pair_gain,
    pair_bias,
    w_up,
    b_up,
    w_down,
    b_down,
):
    rows = layer_input.shape[0]
    parts = lax.axis_size("mp")
    ring = parts // 2
    tokens = rows * lax.axis_size("rows")
    columns = tokens // parts
    core = lax.axis_index("rows")
    z, y = lax.axis_index("mp") // 2, lax.axis_index("mp") % 2

    swap_core = [(0, 1), (1, 0)]
    swap_y = [(m, m ^ 1) for m in range(parts)]

    def rotate_z(by):
        return [(2 * a + b, 2 * ((a + by) % ring) + b) for a in range(ring) for b in range(2)]

    half = HD // 2
    freqs = 10000.0 ** (-jnp.arange(half, dtype=F32) / half)
    positions = core * rows + jnp.arange(rows, dtype=jnp.int32)
    angles = positions.astype(F32)[:, None] * freqs[None, :]
    at = jnp.stack([core, z, y]).astype(jnp.int32)

    w_half = pack_columns(at, w_out, ring)
    w_same = lax.ppermute(w_half, "mp", swap_y)
    queries, own = project(
        layer_input, norm_gain, norm_bias, w_query_key, w_value, jnp.cos(angles), jnp.sin(angles)
    )
    there = lax.ppermute(own, "rows", swap_core)
    passed = [queries]
    for _ in range(1, ring):
        passed.append(lax.ppermute(passed[-1], "mp", rotate_z(1)))
    near, local, *shares = attend(at, queries, own, there, ring, columns)
    sources = [(queries, local)]
    for d in range(1, ring):
        mine = lax.ppermute(shares[d - 1], "mp", rotate_z(d))
        theirs = lax.ppermute(mine, "rows", swap_core)
        sources.append((passed[d], mine, theirs))
    far = lax.ppermute(near, "mp", swap_y)
    w_cross = lax.ppermute(w_same, "rows", swap_core)

    own_maps, other_maps = [], []
    for some in (sources[:-2], sources[-2:-1], sources[-1:]):
        own_side, other_side = pair_maps(at, some, columns)
        own_maps.append(own_side)
        other_maps.append(lax.ppermute(other_side, "mp", swap_y))

    total, *tails = project_out(at, near, far, w_out, w_same, w_cross, ring)
    pair = functools.partial(
        pair_block_fast,
        at,
        own_maps + other_maps,
        w_maps,
        b_maps,
        pair_gain,
        pair_bias,
        w_up,
        b_up,
        w_down,
        b_down,
        float(tokens),
        columns,
    )
    for tail in tails:
        sent = total.astype(BF16)
        total = tail + lax.ppermute(sent, "mp", rotate_z(1)).astype(F32)
    attention = total
    calls = 3
    blocks = rows // 64
    pair_features = None
    for n in range(calls):
        pair_features = pair(first=n * blocks // calls, blocks=blocks // calls, begun=pair_features)
    return (attention, pair_features)


def layer_norm(values, gain, bias):
    average = jnp.mean(values, axis=-1, keepdims=True)
    centered = values - average
    variance = jnp.mean(centered * centered, axis=-1, keepdims=True)
    return centered * lax.rsqrt(variance + 1e-05) * gain + bias


def rotate(values, positions):
    half = values.shape[-1] // 2
    freqs = 10000.0 ** (-jnp.arange(half, dtype=jnp.float32) / half)
    angles = positions.astype(jnp.float32)[:, None] * freqs[None, :]
    cosine = jnp.cos(angles)[:, None, :]
    sine = jnp.sin(angles)[:, None, :]
    lower = values[..., :half]
    upper = values[..., half:]
    return jnp.concatenate([lower * cosine - upper * sine, upper * cosine + lower * sine], axis=-1)


def project_rotated(normed, weight, positions):
    count = normed.shape[0]
    projected = jnp.dot(normed, weight, preferred_element_type=jnp.float32)
    projected = projected.reshape(count, weight.shape[1] // HD, HD)
    return rotate(projected, positions).astype(jnp.bfloat16).reshape(count, weight.shape[1])


def pair_block(maps, w_maps, b_maps, pair_gain, pair_bias, w_up, b_up, w_down, b_down, factor):
    mixed = (
        jnp.einsum("hrc,hp->rcp", maps, w_maps, preferred_element_type=jnp.float32) * factor
        + b_maps
    )
    normed = layer_norm(mixed, pair_gain, pair_bias).astype(jnp.bfloat16)
    hidden = jax.nn.relu(
        jnp.einsum("rcp,pt->rct", normed, w_up, preferred_element_type=jnp.float32) + b_up
    ).astype(jnp.bfloat16)
    return (
        jnp.einsum("rct,tp->rcp", hidden, w_down, preferred_element_type=jnp.float32) + b_down
    ).astype(jnp.bfloat16)


def per_device(
    layer_input,
    norm_gain,
    norm_bias,
    w_query_key,
    w_value,
    w_out,
    w_maps,
    b_maps,
    pair_gain,
    pair_bias,
    w_up,
    b_up,
    w_down,
    b_down,
):
    tok_rows = layer_input.shape[0]
    tokens_all = tok_rows * lax.axis_size("rows")
    local_heads = w_value.shape[1] // HD
    normed = layer_norm(layer_input.astype(jnp.float32), norm_gain, norm_bias).astype(jnp.bfloat16)
    own_positions = lax.axis_index("rows") * tok_rows + jnp.arange(tok_rows, dtype=jnp.int32)
    queries = project_rotated(normed, w_query_key[0], own_positions)
    keys_local = project_rotated(normed, w_query_key[1], own_positions)
    values_local = jnp.dot(normed, w_value, preferred_element_type=jnp.float32).astype(jnp.bfloat16)
    keys_all, values_all = (
        lax.all_gather(keys_local, "rows", axis=0, tiled=True),
        lax.all_gather(values_local, "rows", axis=0, tiled=True),
    )
    head_queries = queries.reshape(tok_rows, local_heads, HD)
    head_keys = keys_all.reshape(tokens_all, local_heads, HD)
    head_values = values_all.reshape(tokens_all, local_heads, HD)
    scores = jnp.einsum(
        "qhd,khd->hqk", head_queries, head_keys, preferred_element_type=jnp.float32
    ) / math.sqrt(HD)
    maps = jax.nn.softmax(scores, axis=-1).astype(jnp.bfloat16)
    context = jnp.einsum("hqk,khd->qhd", maps, head_values, preferred_element_type=jnp.float32)
    context = context.astype(jnp.bfloat16).reshape(tok_rows, local_heads * HD)
    partial_sums = jnp.dot(context, w_out, preferred_element_type=jnp.float32)
    attention = lax.psum_scatter(partial_sums, "mp", scatter_dimension=1, tiled=True)
    factor = float(tokens_all)
    pair_features = pair_block(
        lax.all_to_all(maps, "mp", split_axis=2, concat_axis=0, tiled=True),
        w_maps,
        b_maps,
        pair_gain,
        pair_bias,
        w_up,
        b_up,
        w_down,
        b_down,
        factor,
    )
    return (attention, pair_features)


def solution(mesh):
    in_specs = (
        P(("groups", "rows"), None),
        P(),
        P(),
        P(None, None, "mp"),
        P(None, "mp"),
        P("mp", None),
        P(),
        P(),
        P(),
        P(),
        P(),
        P(),
        P(),
        P(),
    )
    out_specs = (P(("groups", "rows"), "mp"), P(("groups", "rows"), "mp", None))
    if mesh.shape["mp"] != 8 or mesh.shape["rows"] != 2:
        return jax.shard_map(
            per_device, mesh=mesh, in_specs=in_specs, out_specs=out_specs, check_vma=False
        )

    return jax.shard_map(
        per_device_fast, mesh=mesh, in_specs=in_specs, out_specs=out_specs, check_vma=False
    )
```

```python
import functools
import math

import jax
import jax.numpy as jnp
from jax import lax
from jax.experimental import pallas as pl
from jax.experimental.pallas import tpu as pltpu
from jax.sharding import PartitionSpec as P


HD = 128
F32 = jnp.float32
BF16 = jnp.bfloat16
ROOT = math.sqrt(HD)


def params(*axes, mib=24):
    return pltpu.CompilerParams(
        dimension_semantics=axes if axes else None, vmem_limit_bytes=mib * 1024 * 1024
    )


def cost(flops, moved, transcendentals=0):
    return pl.CostEstimate(
        flops=int(flops), bytes_accessed=int(moved), transcendentals=int(transcendentals)
    )


def sds(shape, dtype):
    return jax.ShapeDtypeStruct(shape, dtype)


VMEM = pl.BlockSpec(memory_space=pltpu.VMEM)
ANYWHERE = pl.BlockSpec(memory_space=pl.ANY)
HBM = pl.BlockSpec(memory_space=pltpu.HBM)
SMEM = pl.BlockSpec(memory_space=pltpu.SMEM)


def turn(block, cosine, sine):
    pieces = []
    for head in range(block.shape[1] // HD):
        one = block[:, head * HD : (head + 1) * HD]
        pieces.append(one * cosine + pltpu.roll(one, HD // 2, 1) * sine)
    return jnp.concatenate(pieces, axis=1)


def project_kernel(
    x_ref, gain_ref, bias_ref, wqk_ref, wv_ref, cos_ref, sin_ref, q_ref, kv_ref, x, normed, w, x_sems, w_sems
):
    rows, width = x.shape
    columns = q_ref.shape[1]
    step, chunks, tile = 16, x_sems.shape[0], min(256, columns)
    parts = w_sems.shape[1]
    deep = width // parts
    piece = rows // chunks
    x_copies = [
        pltpu.make_async_copy(
            x_ref.at[n * piece : (n + 1) * piece], x.at[n * piece : (n + 1) * piece], x_sems.at[n]
        )
        for n in range(chunks)
    ]
    sources = (wqk_ref.at[1], wqk_ref.at[0], wv_ref)
    w_copies = [
        pltpu.make_async_copy(
            source.at[n * deep : (n + 1) * deep],
            w.at[which, n * deep : (n + 1) * deep],
            w_sems.at[which, n],
        )
        for which, source in enumerate(sources)
        for n in range(parts)
    ]
    for copy in x_copies + w_copies:
        copy.start()

    def body(i, carry):
        at = pl.ds(pl.multiple_of(i * step, step), step)

        def lanes(n):
            return slice(n * HD, (n + 1) * HD)

        def total(one):
            parts = [jnp.zeros((step, HD), F32) for _ in range(4)]
            for n in range(width // HD):
                parts[n % 4] = parts[n % 4] + one(x[at, lanes(n)].astype(F32))
            whole = (parts[0] + parts[1]) + (parts[2] + parts[3])
            return jnp.sum(whole, axis=1, keepdims=True) * (1.0 / width)

        mean = total(lambda v: v)
        variance = total(lambda v: (v - mean) * (v - mean))
        scale = lax.rsqrt(variance + 1e-05)
        for n in range(width // HD):
            scaled = (x[at, lanes(n)].astype(F32) - mean) * scale
            normed[at, lanes(n)] = (scaled * gain_ref[:, lanes(n)] + bias_ref[:, lanes(n)]).astype(BF16)
        return carry

    for n in range(chunks):
        x_copies[n].wait()
        lax.fori_loop(n * piece // step, (n + 1) * piece // step, body, 0, unroll=2)
    cosine = jnp.concatenate([cos_ref[...], cos_ref[...]], axis=1)
    sine = jnp.concatenate([-sin_ref[...], sin_ref[...]], axis=1)
    for which in range(3):
        for n in range(parts):
            w_copies[which * parts + n].wait()
        for n in range(columns // tile):
            block = jnp.dot(
                normed[...], w[which, :, n * tile : (n + 1) * tile], preferred_element_type=F32
            )
            if which < 2:
                block = turn(block, cosine, sine)
            at = n * tile
            if which == 0:
                kv_ref[:, at : at + tile] = block.astype(BF16)
            elif which == 1:
                q_ref[:, at : at + tile] = block.astype(BF16)
            else:
                kv_ref[:, columns + at : columns + at + tile] = block.astype(BF16)


def project(x, gain, bias, w_query_key, w_value, cosine, sine):
    rows, width = x.shape
    columns = w_value.shape[1]
    return pl.pallas_call(
        project_kernel,
        in_specs=[HBM, VMEM, VMEM, HBM, HBM, VMEM, VMEM],
        out_specs=[VMEM, VMEM],
        out_shape=[sds((rows, columns), BF16), sds((rows, 2 * columns), BF16)],
        scratch_shapes=[
            pltpu.VMEM((rows, width), BF16),
            pltpu.VMEM((rows, width), BF16),
            pltpu.VMEM((3, width, columns), BF16),
            pltpu.SemaphoreType.DMA((4,)),
            pltpu.SemaphoreType.DMA((3, 2)),
        ],
        compiler_params=params(mib=44),
        cost_estimate=cost(6 * rows * width * columns, 2 * width * (rows + 3 * columns)),
        name="project",
    )(x, gain.reshape(1, width), bias.reshape(1, width), w_query_key, w_value, cosine, sine)


def attend_kernel(
    ring, at_ref, q_ref, own_ref, there_ref, context_ref, local_ref, *rest
):
    share_refs, level_ref = rest[:-1], rest[-1]
    rows, width = q_ref.shape
    heads = width // HD
    columns = local_ref.shape[0] // 2 - 8
    core, z, y = at_ref[0], at_ref[1], at_ref[2]
    lane = lax.broadcasted_iota(jnp.int32, (rows, HD), 1)
    table = jnp.zeros((rows, HD), F32)
    contract = (((1,), (1,)), ((), ()))
    for head in range(heads):
        at = slice(head * HD, (head + 1) * HD)
        at_v = slice(width + head * HD, width + (head + 1) * HD)
        scores = [
            lax.dot_general(q_ref[:, at], ref[:, at], contract, preferred_element_type=F32)
            * (1.0 / ROOT)
            for ref in (own_ref, there_ref)
        ]
        top = jnp.max(jnp.maximum(scores[0], scores[1]), axis=1, keepdims=True)
        raised = [jnp.exp(part - top) for part in scores]
        total = jnp.sum(raised[0] + raised[1], axis=1, keepdims=True)
        inverse = 1.0 / total
        maps = [(part * inverse).astype(BF16) for part in raised]
        context_ref[:, at] = (
            jnp.dot(maps[0], own_ref[:, at_v], preferred_element_type=F32)
            + jnp.dot(maps[1], there_ref[:, at_v], preferred_element_type=F32)
        ).astype(BF16)
        level = (top + jnp.log(total)) * ROOT
        high = level.astype(BF16).astype(F32)
        middle = (level - high).astype(BF16).astype(F32)
        low = (level - high - middle).astype(BF16).astype(F32)
        for piece, part in enumerate((high, middle, low)):
            table = jnp.where(lane == 3 * head + piece, part, table)
    level_ref[...] = jnp.zeros_like(level_ref)
    level_ref[:, 0:rows] = table.T[0:16].astype(BF16)

    def key_rows(chip, which):
        token = chip * (2 * columns) + which * columns
        holder = (token >= rows).astype(jnp.int32)
        start = pl.ds(pl.multiple_of(token - holder * rows, 32), columns)
        mine = (holder == core).astype(F32)
        near = own_ref[start, 0:width].astype(F32)
        far = there_ref[start, 0:width].astype(F32)
        return (near * mine + far * (1.0 - mine)).astype(BF16)

    local_ref[0:columns, :] = key_rows(z, y)
    local_ref[columns : 2 * columns, :] = key_rows(z, 1 - y)
    local_ref[2 * columns : 2 * columns + 16, :] = level_ref[...]
    for distance, share_ref in enumerate(share_refs, 1):
        chip = lax.rem(z + distance, ring)
        share_ref[0:columns, :] = key_rows(chip, core)
        share_ref[columns : columns + 16, :] = level_ref[...]


def attend(at, queries, own, there, ring, columns):
    rows, width = queries.shape
    tokens = 2 * rows
    return pl.pallas_call(
        functools.partial(attend_kernel, ring),
        in_specs=[SMEM, VMEM, VMEM, VMEM],
        out_specs=[VMEM] * (ring + 1),
        out_shape=[sds((rows, width), BF16), sds((2 * columns + 16, width), BF16)]
        + [sds((columns + 16, width), BF16)] * (ring - 1),
        scratch_shapes=[pltpu.VMEM((16, width), BF16)],
        compiler_params=params(),
        cost_estimate=cost(4 * rows * tokens * width, 8 * rows * width, rows * tokens * width // HD),
        name="attend",
    )(at, queries, own, there)


def pack_kernel(count, at_ref, w_ref, out_ref, sems):
    depth, wide = out_ref.shape
    tile = wide // count
    core, z, y = at_ref[0], at_ref[1], at_ref[2]
    copies = []
    piece = depth // sems.shape[1]
    for n in range(count):
        block = 2 * lax.rem(z + (2 * count - 1 - n), count) + 1 - y
        for part in range(sems.shape[1]):
            copies.append(
                pltpu.make_async_copy(
                    w_ref.at[
                        pl.ds(pl.multiple_of(core * depth + part * piece, piece), piece),
                        pl.ds(pl.multiple_of(block * tile, tile), tile),
                    ],
                    out_ref.at[part * piece : (part + 1) * piece, n * tile : (n + 1) * tile],
                    sems.at[n, part],
                )
            )
    for copy in copies:
        copy.start()
    for copy in copies:
        copy.wait()


def pack_columns(at, w, count):
    depth, wide = w.shape[0] // 2, w.shape[1] // 2
    return pl.pallas_call(
        functools.partial(pack_kernel, count),
        in_specs=[SMEM, HBM],
        out_specs=VMEM,
        out_shape=sds((depth, wide), BF16),
        scratch_shapes=[pltpu.SemaphoreType.DMA((count, 4))],
        compiler_params=params(),
        cost_estimate=cost(0, 4 * depth * wide),
        name="pack_columns",
    )(at, w)


def project_out_kernel(at_ref, near_ref, far_ref, w_ref, w_same_ref, w_cross_ref, *rest):
    out_refs, (w, sems) = rest[:-2], rest[-2:]
    count = len(out_refs)
    tile = out_refs[0].shape[1]
    half = w_same_ref.shape[0]
    core, z, y = at_ref[0], at_ref[1], at_ref[2]
    copies = []
    for n in range(count):
        block = 2 * lax.rem(z + (2 * count - 1 - n), count) + y
        copies.append(
            pltpu.make_async_copy(
                w_ref.at[:, pl.ds(pl.multiple_of(block * tile, tile), tile)], w.at[n], sems.at[n]
            )
        )
    for copy in copies:
        copy.start()
    same = far_ref[:, pl.ds(pl.multiple_of(core * half, half), half)]
    cross = far_ref[:, pl.ds(pl.multiple_of((1 - core) * half, half), half)]
    for n, out_ref in enumerate(out_refs):
        lanes = slice(n * tile, (n + 1) * tile)
        block = jnp.dot(same, w_same_ref[:, lanes], preferred_element_type=F32) + jnp.dot(
            cross, w_cross_ref[:, lanes], preferred_element_type=F32
        )
        copies[n].wait()
        block = block + jnp.dot(near_ref[...], w[n], preferred_element_type=F32)
        out_ref[...] = block.astype(out_ref.dtype)


def project_out(at, near, far, w, w_same, w_cross, count):
    rows, depth = near.shape
    _, wide = w_same.shape
    tile = wide // count
    return pl.pallas_call(
        project_out_kernel,
        in_specs=[SMEM, VMEM, VMEM, ANYWHERE, VMEM, VMEM],
        out_specs=[VMEM] * count,
        out_shape=[sds((rows, tile), BF16)] + [sds((rows, tile), F32)] * (count - 1),
        scratch_shapes=[
            pltpu.VMEM((count, depth, tile), BF16),
            pltpu.SemaphoreType.DMA((count,)),
        ],
        compiler_params=params(),
        cost_estimate=cost(4 * rows * depth * wide, 4 * wide * (rows + depth)),
        name="project_out",
    )(at, near, far, w, w_same, w_cross)


def pair_maps_kernel(sources, first, at_ref, *refs):
    own_ref, other_ref = refs[-2:]
    rows = own_ref.shape[1]
    width = refs[0].shape[1]
    heads = width // HD
    wide = own_ref.shape[2]
    columns = wide // heads
    lane_head = lax.broadcasted_iota(jnp.int32, (columns, width), 1) // HD
    row = lax.broadcasted_iota(jnp.int32, (16, wide), 0)
    column = lax.broadcasted_iota(jnp.int32, (16, wide), 1)
    hit = jnp.zeros((16, wide), jnp.bool_)
    for head in range(heads):
        inside = (column >= head * columns) & (column < (head + 1) * columns)
        hit = hit | (inside & (row >= 3 * head) & (row < 3 * head + 3))
    pick = jnp.where(hit, -1.0, 0.0).astype(BF16)
    straight = (at_ref[2] == at_ref[0]).astype(F32)
    taken = 0
    for place, count in enumerate(sources):
        q_ref, keys = refs[taken], refs[taken + 1 : taken + count]
        taken += count
        if count == 2:
            pieces = [keys[0][n * columns : (n + 1) * columns, :].astype(F32) for n in range(2)]
            levels = keys[0][2 * columns : 2 * columns + 16, first : first + rows]
        else:
            mine = keys[0][0:columns, :].astype(F32)
            theirs = keys[1][0:columns, :].astype(F32)
            pieces = [
                mine * straight + theirs * (1.0 - straight),
                theirs * straight + mine * (1.0 - straight),
            ]
            levels = keys[0][columns : columns + 16, first : first + rows]
        level = lax.dot_general(
            levels, pick, (((0,), (0,)), ((), ())), preferred_element_type=F32
        )
        for k, out_ref in zip(pieces, (own_ref, other_ref)):
            spread = jnp.concatenate(
                [jnp.where(lane_head == head, k, 0.0).astype(BF16) for head in range(heads)], axis=0
            )
            scores = lax.dot_general(
                q_ref[...], spread, (((1,), (1,)), ((), ())), preferred_element_type=F32
            )
            out_ref[place] = jnp.exp((scores + level) * (1.0 / ROOT)).astype(BF16)


def pair_maps(at, sources, columns, first=0):
    rows, width = sources[0][0].shape
    wide = (width // HD) * columns
    count = len(sources)
    flat = [array for source in sources for array in source]
    return pl.pallas_call(
        functools.partial(pair_maps_kernel, [len(source) for source in sources], first),
        in_specs=[SMEM] + [VMEM] * len(flat),
        out_specs=[VMEM] * 2,
        out_shape=[sds((count, rows, wide), BF16)] * 2,
        compiler_params=params(),
        cost_estimate=cost(
            4 * count * rows * wide * width, 8 * count * rows * wide, 2 * count * rows * wide
        ),
        name="pair_maps",
    )(at, *flat)


def pair_kernel(factor, inputs, count, chained, at_ref, *refs):
    maps_refs = refs[:inputs]
    (w_maps_ref, b_maps_ref, gain_ref, bias_ref, w_up_ref, b_up_ref, w_down_ref, b_down_ref) = refs[
        inputs : inputs + 8
    ]
    out_ref, spread_ref, up_ref, shift_ref, rows_ref = refs[inputs + 8 + chained :]
    block = out_ref.shape[0]
    columns = out_ref.shape[1]
    chunk = 8 * columns
    channels = out_ref.shape[2]
    heads_all = w_maps_ref.shape[0]
    heads = heads_all // count
    group = HD // heads_all

    @pl.when(pl.program_id(0) == 0)
    def _():
        row = lax.broadcasted_iota(jnp.int32, (heads_all, heads_all), 0)
        column = lax.broadcasted_iota(jnp.int32, (heads_all, heads_all), 1)
        ring = count // 2
        distance = lax.rem(row // heads, ring)
        chip = lax.rem(at_ref[1] + ring - distance, ring)
        side = jnp.where(row // heads >= ring, 1 - at_ref[2], at_ref[2])
        head = (2 * chip + side) * heads + lax.rem(row, heads)
        sort = jnp.where(column == head, 1.0, 0.0).astype(BF16)
        w = jnp.dot(sort, w_maps_ref[...], preferred_element_type=F32)
        w = (w - jnp.sum(w, axis=1, keepdims=True) * (1.0 / channels)) * factor
        high = w.astype(BF16)
        low = (w - high.astype(F32)).astype(BF16)
        spread_ref[...] = jnp.zeros_like(spread_ref)
        for i in range(group):
            at = slice(i * channels, (i + 1) * channels)
            spread_ref[i * heads_all : (i + 1) * heads_all, at] = high
            spread_ref[HD + i * heads_all : HD + (i + 1) * heads_all, at] = low
        b = b_maps_ref[...]
        b = b - jnp.sum(b, axis=1, keepdims=True) * (1.0 / channels)
        shift_ref[...] = jnp.concatenate([b] * group, axis=1)
        up_ref[0:channels, :] = w_up_ref[...]
        b_up = b_up_ref[...]
        top = b_up.astype(BF16).astype(F32)
        middle = (b_up - top).astype(BF16).astype(F32)
        tail = jnp.concatenate(
            [top, middle, b_up - top - middle, jnp.zeros((channels - 3, b_up.shape[1]), F32)], axis=0
        )
        up_ref[channels : 2 * channels, :] = tail.astype(BF16)
        rows_ref[...] = jnp.zeros_like(rows_ref)

    def fill():
        lots = [(ref, n) for ref in maps_refs for n in range(ref.shape[0])]
        for source, (ref, n) in enumerate(lots):
            wide = ref[n].astype(F32)
            for head in range(heads):
                place = (source * heads + head) * block
                rows_ref[place : place + block, 0:columns] = wide[
                    :, head * columns : (head + 1) * columns
                ]

    gain, bias = gain_ref[...], bias_ref[...]

    def normalise(g):
        tall = jnp.concatenate(
            [rows_ref[pl.ds(g * group + i, heads_all, stride=block), :] for i in range(group)], axis=0
        )
        flat = tall.T[0:columns].astype(BF16)
        mixed = (
            jnp.dot(
                jnp.concatenate([flat, flat], axis=1), spread_ref[...], preferred_element_type=F32
            )
            + shift_ref[...]
        )
        pieces = []
        for i in range(group):
            centered = mixed[:, i * channels : (i + 1) * channels]
            variance = jnp.sum(centered * centered, axis=1, keepdims=True) * (1.0 / channels)
            pieces.append((centered * lax.rsqrt(variance + 1e-05) * gain + bias).astype(BF16))
        return jnp.concatenate(pieces, axis=0)

    lane = lax.broadcasted_iota(jnp.int32, (chunk, channels), 1)
    unit = jnp.where(lane < 3, 1.0, 0.0).astype(BF16)

    def transition(normed, at):
        hidden = jnp.dot(
            jnp.concatenate([normed, unit], axis=1), up_ref[...], preferred_element_type=F32
        )
        hidden = jnp.maximum(hidden, 0.0).astype(BF16)
        result = jnp.dot(hidden, w_down_ref[...], preferred_element_type=F32) + b_down_ref[...]
        result = result.astype(BF16)
        for i in range(chunk // columns):
            out_ref[at + i] = result[i * columns : (i + 1) * columns]

    fill()
    per = chunk // columns // group
    waiting = None
    for first in range(0, block // group, per):
        normed = jnp.concatenate([normalise(g) for g in range(first, first + per)], axis=0)
        if waiting is not None:
            transition(*waiting)
        waiting = (normed, first * group)
    transition(*waiting)


def pair_block_fast(
    at,
    maps,
    w_maps,
    b_maps,
    pair_gain,
    pair_bias,
    w_up,
    b_up,
    w_down,
    b_down,
    factor,
    columns,
    block=64,
    first=0,
    blocks=None,
    begun=None,
):
    count = sum(array.shape[0] for array, _ in maps)
    rows, wide = maps[0][0].shape[1:]
    channels, hidden = w_up.shape
    heads_all = w_maps.shape[0]
    group = HD // heads_all
    whole = lambda *shape: pl.BlockSpec(shape, lambda n: (0,) * len(shape))
    blocks = rows // block if blocks is None else blocks
    pairs = blocks * block * columns
    chained = [] if begun is None else [begun]
    return pl.pallas_call(
        functools.partial(pair_kernel, factor, len(maps), count, len(chained)),
        grid=(blocks,),
        in_specs=[SMEM]
        + [
            pl.BlockSpec(
                (array.shape[0], block, wide),
                lambda n, skipped=skipped: (0, first + n - skipped // block, 0),
            )
            for array, skipped in maps
        ]
        + [
            whole(heads_all, channels),
            whole(1, channels),
            whole(1, channels),
            whole(1, channels),
            whole(channels, hidden),
            whole(1, hidden),
            whole(hidden, channels),
            whole(1, channels),
        ]
        + [pl.BlockSpec(memory_space=pl.ANY)] * len(chained),
        out_specs=pl.BlockSpec((block, columns, channels), lambda n: (first + n, 0, 0)),
        out_shape=sds((rows, columns, channels), BF16),
        scratch_shapes=[
            pltpu.VMEM((2 * HD, group * channels), BF16),
            pltpu.VMEM((2 * channels, hidden), BF16),
            pltpu.VMEM((1, group * channels), F32),
            pltpu.VMEM((heads_all * block, HD), F32),
        ],
        input_output_aliases={len(maps) + 9: 0} if chained else {},
        compiler_params=params("arbitrary"),
        cost_estimate=cost(4 * pairs * channels * hidden, 4 * pairs * channels, pairs * channels),
        name="pair_block",
    )(
        at,
        *[array for array, _ in maps],
        w_maps,
        b_maps.reshape(1, -1),
        pair_gain.reshape(1, -1),
        pair_bias.reshape(1, -1),
        w_up,
        b_up.reshape(1, -1),
        w_down,
        b_down.reshape(1, -1),
        *chained,
    )


def per_device_fast(
    layer_input,
    norm_gain,
    norm_bias,
    w_query_key,
    w_value,
    w_out,
    w_maps,
    b_maps,
    pair_gain,
    pair_bias,
    w_up,
    b_up,
    w_down,
    b_down,
):
    rows = layer_input.shape[0]
    parts = lax.axis_size("mp")
    ring = parts // 2
    tokens = rows * lax.axis_size("rows")
    columns = tokens // parts
    core = lax.axis_index("rows")
    z, y = lax.axis_index("mp") // 2, lax.axis_index("mp") % 2

    swap_core = [(0, 1), (1, 0)]
    swap_y = [(m, m ^ 1) for m in range(parts)]

    def rotate_z(by):
        return [(2 * a + b, 2 * ((a + by) % ring) + b) for a in range(ring) for b in range(2)]

    half = HD // 2
    freqs = 10000.0 ** (-jnp.arange(half, dtype=F32) / half)
    positions = core * rows + jnp.arange(rows, dtype=jnp.int32)
    angles = positions.astype(F32)[:, None] * freqs[None, :]
    at = jnp.stack([core, z, y]).astype(jnp.int32)

    w_half = pack_columns(at, w_out, ring)
    w_same = lax.ppermute(w_half, "mp", swap_y)
    queries, own = project(
        layer_input, norm_gain, norm_bias, w_query_key, w_value, jnp.cos(angles), jnp.sin(angles)
    )
    there = lax.ppermute(own, "rows", swap_core)
    passed = [queries]
    for _ in range(1, ring - 1):
        passed.append(lax.ppermute(passed[-1], "mp", rotate_z(1)))
    calls = 3
    cut = rows // calls
    last = [lax.ppermute(part, "mp", rotate_z(1)) for part in (passed[-1][:cut], passed[-1][cut:])]
    near, local, *shares = attend(at, queries, own, there, ring, columns)
    sources = [(queries, local)]
    for d in range(1, ring):
        mine = lax.ppermute(shares[d - 1], "mp", rotate_z(d))
        theirs = lax.ppermute(mine, "rows", swap_core)
        if d < ring - 1:
            sources.append((passed[d], mine, theirs))
    far = lax.ppermute(near, "mp", swap_y)
    w_cross = lax.ppermute(w_same, "rows", swap_core)

    own_maps, other_maps = [], []
    for some, start in (
        (sources[:-1], 0),
        (sources[-1:], 0),
        ([(last[0], mine, theirs)], 0),
        ([(last[1], mine, theirs)], cut),
    ):
        own_side, other_side = pair_maps(at, some, columns, start)
        own_maps.append((own_side, start))
        other_maps.append((lax.ppermute(other_side, "mp", swap_y), start))

    total, *tails = project_out(at, near, far, w_out, w_same, w_cross, ring)
    pair = functools.partial(
        pair_block_fast,
        at,
        w_maps=w_maps,
        b_maps=b_maps,
        pair_gain=pair_gain,
        pair_bias=pair_bias,
        w_up=w_up,
        b_up=b_up,
        w_down=w_down,
        b_down=b_down,
        factor=float(tokens),
        columns=columns,
    )
    for tail in tails:
        sent = total.astype(BF16)
        total = tail + lax.ppermute(sent, "mp", rotate_z(1)).astype(F32)
    attention = total
    blocks = rows // 64
    pair_features = None
    for n in range(calls):
        pair_features = pair(
            [side[k] for side in (own_maps, other_maps) for k in (0, 1, 2 if n == 0 else 3)],
            first=n * blocks // calls,
            blocks=blocks // calls,
            begun=pair_features,
        )
    return (attention, pair_features)


def layer_norm(values, gain, bias):
    average = jnp.mean(values, axis=-1, keepdims=True)
    centered = values - average
    variance = jnp.mean(centered * centered, axis=-1, keepdims=True)
    return centered * lax.rsqrt(variance + 1e-05) * gain + bias


def rotate(values, positions):
    half = values.shape[-1] // 2
    freqs = 10000.0 ** (-jnp.arange(half, dtype=jnp.float32) / half)
    angles = positions.astype(jnp.float32)[:, None] * freqs[None, :]
    cosine = jnp.cos(angles)[:, None, :]
    sine = jnp.sin(angles)[:, None, :]
    lower = values[..., :half]
    upper = values[..., half:]
    return jnp.concatenate([lower * cosine - upper * sine, upper * cosine + lower * sine], axis=-1)


def project_rotated(normed, weight, positions):
    count = normed.shape[0]
    projected = jnp.dot(normed, weight, preferred_element_type=jnp.float32)
    projected = projected.reshape(count, weight.shape[1] // HD, HD)
    return rotate(projected, positions).astype(jnp.bfloat16).reshape(count, weight.shape[1])


def pair_block(maps, w_maps, b_maps, pair_gain, pair_bias, w_up, b_up, w_down, b_down, factor):
    mixed = (
        jnp.einsum("hrc,hp->rcp", maps, w_maps, preferred_element_type=jnp.float32) * factor
        + b_maps
    )
    normed = layer_norm(mixed, pair_gain, pair_bias).astype(jnp.bfloat16)
    hidden = jax.nn.relu(
        jnp.einsum("rcp,pt->rct", normed, w_up, preferred_element_type=jnp.float32) + b_up
    ).astype(jnp.bfloat16)
    return (
        jnp.einsum("rct,tp->rcp", hidden, w_down, preferred_element_type=jnp.float32) + b_down
    ).astype(jnp.bfloat16)


def per_device(
    layer_input,
    norm_gain,
    norm_bias,
    w_query_key,
    w_value,
    w_out,
    w_maps,
    b_maps,
    pair_gain,
    pair_bias,
    w_up,
    b_up,
    w_down,
    b_down,
):
    tok_rows = layer_input.shape[0]
    tokens_all = tok_rows * lax.axis_size("rows")
    local_heads = w_value.shape[1] // HD
    normed = layer_norm(layer_input.astype(jnp.float32), norm_gain, norm_bias).astype(jnp.bfloat16)
    own_positions = lax.axis_index("rows") * tok_rows + jnp.arange(tok_rows, dtype=jnp.int32)
    queries = project_rotated(normed, w_query_key[0], own_positions)
    keys_local = project_rotated(normed, w_query_key[1], own_positions)
    values_local = jnp.dot(normed, w_value, preferred_element_type=jnp.float32).astype(jnp.bfloat16)
    keys_all, values_all = (
        lax.all_gather(keys_local, "rows", axis=0, tiled=True),
        lax.all_gather(values_local, "rows", axis=0, tiled=True),
    )
    head_queries = queries.reshape(tok_rows, local_heads, HD)
    head_keys = keys_all.reshape(tokens_all, local_heads, HD)
    head_values = values_all.reshape(tokens_all, local_heads, HD)
    scores = jnp.einsum(
        "qhd,khd->hqk", head_queries, head_keys, preferred_element_type=jnp.float32
    ) / math.sqrt(HD)
    maps = jax.nn.softmax(scores, axis=-1).astype(jnp.bfloat16)
    context = jnp.einsum("hqk,khd->qhd", maps, head_values, preferred_element_type=jnp.float32)
    context = context.astype(jnp.bfloat16).reshape(tok_rows, local_heads * HD)
    partial_sums = jnp.dot(context, w_out, preferred_element_type=jnp.float32)
    attention = lax.psum_scatter(partial_sums, "mp", scatter_dimension=1, tiled=True)
    factor = float(tokens_all)
    pair_features = pair_block(
        lax.all_to_all(maps, "mp", split_axis=2, concat_axis=0, tiled=True),
        w_maps,
        b_maps,
        pair_gain,
        pair_bias,
        w_up,
        b_up,
        w_down,
        b_down,
        factor,
    )
    return (attention, pair_features)


def solution(mesh):
    in_specs = (
        P(("groups", "rows"), None),
        P(),
        P(),
        P(None, None, "mp"),
        P(None, "mp"),
        P("mp", None),
        P(),
        P(),
        P(),
        P(),
        P(),
        P(),
        P(),
        P(),
    )
    out_specs = (P(("groups", "rows"), "mp"), P(("groups", "rows"), "mp", None))
    if mesh.shape["mp"] != 8 or mesh.shape["rows"] != 2:
        return jax.shard_map(
            per_device, mesh=mesh, in_specs=in_specs, out_specs=out_specs, check_vma=False
        )

    return jax.shard_map(
        per_device_fast, mesh=mesh, in_specs=in_specs, out_specs=out_specs, check_vma=False
    )
```

```python
import functools
import math

import jax
import jax.numpy as jnp
from jax import lax
from jax.experimental import pallas as pl
from jax.experimental.pallas import tpu as pltpu
from jax.sharding import PartitionSpec as P


HD = 128
F32 = jnp.float32
BF16 = jnp.bfloat16
ROOT = math.sqrt(HD)


def params(*axes, mib=24):
    return pltpu.CompilerParams(
        dimension_semantics=axes if axes else None, vmem_limit_bytes=mib * 1024 * 1024
    )


def cost(flops, moved, transcendentals=0):
    return pl.CostEstimate(
        flops=int(flops), bytes_accessed=int(moved), transcendentals=int(transcendentals)
    )


def sds(shape, dtype):
    return jax.ShapeDtypeStruct(shape, dtype)


def chip_at(place):
    return place + lax.div(place, 2) * (1 - 2 * lax.rem(place, 2))


VMEM = pl.BlockSpec(memory_space=pltpu.VMEM)
ANYWHERE = pl.BlockSpec(memory_space=pl.ANY)
HBM = pl.BlockSpec(memory_space=pltpu.HBM)
SMEM = pl.BlockSpec(memory_space=pltpu.SMEM)


def turn(block, cosine, sine):
    pieces = []
    for head in range(block.shape[1] // HD):
        one = block[:, head * HD : (head + 1) * HD]
        pieces.append(one * cosine + pltpu.roll(one, HD // 2, 1) * sine)
    return jnp.concatenate(pieces, axis=1)


def project_kernel(
    x_ref, gain_ref, bias_ref, wqk_ref, wv_ref, cos_ref, sin_ref, q_ref, kv_ref, x, normed, w, x_sems, w_sems
):
    rows, width = x.shape
    columns = q_ref.shape[1]
    step, chunks, tile = 16, x_sems.shape[0], min(256, columns)
    parts = w_sems.shape[1]
    deep = width // parts
    piece = rows // chunks
    x_copies = [
        pltpu.make_async_copy(
            x_ref.at[n * piece : (n + 1) * piece], x.at[n * piece : (n + 1) * piece], x_sems.at[n]
        )
        for n in range(chunks)
    ]
    sources = (wqk_ref.at[1], wqk_ref.at[0], wv_ref)
    w_copies = [
        pltpu.make_async_copy(
            source.at[n * deep : (n + 1) * deep],
            w.at[which, n * deep : (n + 1) * deep],
            w_sems.at[which, n],
        )
        for which, source in enumerate(sources)
        for n in range(parts)
    ]
    for copy in x_copies + w_copies:
        copy.start()

    def body(i, carry):
        at = pl.ds(pl.multiple_of(i * step, step), step)

        def lanes(n):
            return slice(n * HD, (n + 1) * HD)

        def total(one):
            parts = [jnp.zeros((step, HD), F32) for _ in range(4)]
            for n in range(width // HD):
                parts[n % 4] = parts[n % 4] + one(x[at, lanes(n)].astype(F32))
            whole = (parts[0] + parts[1]) + (parts[2] + parts[3])
            return jnp.sum(whole, axis=1, keepdims=True) * (1.0 / width)

        mean = total(lambda v: v)
        variance = total(lambda v: (v - mean) * (v - mean))
        scale = lax.rsqrt(variance + 1e-05)
        for n in range(width // HD):
            scaled = (x[at, lanes(n)].astype(F32) - mean) * scale
            normed[at, lanes(n)] = (scaled * gain_ref[:, lanes(n)] + bias_ref[:, lanes(n)]).astype(BF16)
        return carry

    for n in range(chunks):
        x_copies[n].wait()
        lax.fori_loop(n * piece // step, (n + 1) * piece // step, body, 0, unroll=2)
    cosine = jnp.concatenate([cos_ref[...], cos_ref[...]], axis=1)
    sine = jnp.concatenate([-sin_ref[...], sin_ref[...]], axis=1)
    for which in range(3):
        for n in range(parts):
            w_copies[which * parts + n].wait()
        for n in range(columns // tile):
            block = jnp.dot(
                normed[...], w[which, :, n * tile : (n + 1) * tile], preferred_element_type=F32
            )
            if which < 2:
                block = turn(block, cosine, sine)
            at = n * tile
            if which == 0:
                kv_ref[:, at : at + tile] = block.astype(BF16)
            elif which == 1:
                q_ref[:, at : at + tile] = block.astype(BF16)
            else:
                kv_ref[:, columns + at : columns + at + tile] = block.astype(BF16)


def project(x, gain, bias, w_query_key, w_value, cosine, sine):
    rows, width = x.shape
    columns = w_value.shape[1]
    return pl.pallas_call(
        project_kernel,
        in_specs=[HBM, VMEM, VMEM, HBM, HBM, VMEM, VMEM],
        out_specs=[VMEM, VMEM],
        out_shape=[sds((rows, columns), BF16), sds((rows, 2 * columns), BF16)],
        scratch_shapes=[
            pltpu.VMEM((rows, width), BF16),
            pltpu.VMEM((rows, width), BF16),
            pltpu.VMEM((3, width, columns), BF16),
            pltpu.SemaphoreType.DMA((4,)),
            pltpu.SemaphoreType.DMA((3, 2)),
        ],
        compiler_params=params(mib=44),
        cost_estimate=cost(6 * rows * width * columns, 2 * width * (rows + 3 * columns)),
        name="project",
    )(x, gain.reshape(1, width), bias.reshape(1, width), w_query_key, w_value, cosine, sine)


def attend_kernel(
    ring, at_ref, q_ref, own_ref, there_ref, context_ref, local_ref, *rest
):
    share_refs, level_ref = rest[:-1], rest[-1]
    rows, width = q_ref.shape
    heads = width // HD
    columns = local_ref.shape[0] // 2 - 8
    core, z, y = at_ref[0], at_ref[1], at_ref[2]
    lane = lax.broadcasted_iota(jnp.int32, (rows, HD), 1)
    table = jnp.zeros((rows, HD), F32)
    contract = (((1,), (1,)), ((), ()))
    for head in range(heads):
        at = slice(head * HD, (head + 1) * HD)
        at_v = slice(width + head * HD, width + (head + 1) * HD)
        scores = [
            lax.dot_general(q_ref[:, at], ref[:, at], contract, preferred_element_type=F32)
            * (1.0 / ROOT)
            for ref in (own_ref, there_ref)
        ]
        top = jnp.max(jnp.maximum(scores[0], scores[1]), axis=1, keepdims=True)
        raised = [jnp.exp(part - top) for part in scores]
        total = jnp.sum(raised[0] + raised[1], axis=1, keepdims=True)
        inverse = 1.0 / total
        maps = [(part * inverse).astype(BF16) for part in raised]
        context_ref[:, at] = (
            jnp.dot(maps[0], own_ref[:, at_v], preferred_element_type=F32)
            + jnp.dot(maps[1], there_ref[:, at_v], preferred_element_type=F32)
        ).astype(BF16)
        level = (top + jnp.log(total)) * ROOT
        high = level.astype(BF16).astype(F32)
        middle = (level - high).astype(BF16).astype(F32)
        low = (level - high - middle).astype(BF16).astype(F32)
        for piece, part in enumerate((high, middle, low)):
            table = jnp.where(lane == 3 * head + piece, part, table)
    level_ref[...] = jnp.zeros_like(level_ref)
    level_ref[:, 0:rows] = table.T[0:16].astype(BF16)

    def key_rows(chip, which):
        token = chip * (2 * columns) + which * columns
        holder = (token >= rows).astype(jnp.int32)
        start = pl.ds(pl.multiple_of(token - holder * rows, 32), columns)
        mine = (holder == core).astype(F32)
        near = own_ref[start, 0:width].astype(F32)
        far = there_ref[start, 0:width].astype(F32)
        return (near * mine + far * (1.0 - mine)).astype(BF16)

    local_ref[0:columns, :] = key_rows(chip_at(z), y)
    local_ref[columns : 2 * columns, :] = key_rows(chip_at(z), 1 - y)
    local_ref[2 * columns : 2 * columns + 16, :] = level_ref[...]
    for distance, share_ref in enumerate(share_refs, 1):
        chip = chip_at(lax.rem(z + distance, ring))
        share_ref[0:columns, :] = key_rows(chip, core)
        share_ref[columns : columns + 16, :] = level_ref[...]


def attend(at, queries, own, there, ring, columns):
    rows, width = queries.shape
    tokens = 2 * rows
    return pl.pallas_call(
        functools.partial(attend_kernel, ring),
        in_specs=[SMEM, VMEM, VMEM, VMEM],
        out_specs=[VMEM] * (ring + 1),
        out_shape=[sds((rows, width), BF16), sds((2 * columns + 16, width), BF16)]
        + [sds((columns + 16, width), BF16)] * (ring - 1),
        scratch_shapes=[pltpu.VMEM((16, width), BF16)],
        compiler_params=params(),
        cost_estimate=cost(4 * rows * tokens * width, 8 * rows * width, rows * tokens * width // HD),
        name="attend",
    )(at, queries, own, there)


def pack_kernel(count, at_ref, w_ref, out_ref, sems):
    depth, wide = out_ref.shape
    tile = wide // count
    core, z, y = at_ref[0], at_ref[1], at_ref[2]
    copies = []
    piece = depth // sems.shape[1]
    for n in range(count):
        block = 2 * chip_at(lax.rem(z + (2 * count - 1 - n), count)) + 1 - y
        for part in range(sems.shape[1]):
            copies.append(
                pltpu.make_async_copy(
                    w_ref.at[
                        pl.ds(pl.multiple_of(core * depth + part * piece, piece), piece),
                        pl.ds(pl.multiple_of(block * tile, tile), tile),
                    ],
                    out_ref.at[part * piece : (part + 1) * piece, n * tile : (n + 1) * tile],
                    sems.at[n, part],
                )
            )
    for copy in copies:
        copy.start()
    for copy in copies:
        copy.wait()


def pack_columns(at, w, count):
    depth, wide = w.shape[0] // 2, w.shape[1] // 2
    return pl.pallas_call(
        functools.partial(pack_kernel, count),
        in_specs=[SMEM, HBM],
        out_specs=VMEM,
        out_shape=sds((depth, wide), BF16),
        scratch_shapes=[pltpu.SemaphoreType.DMA((count, 4))],
        compiler_params=params(),
        cost_estimate=cost(0, 4 * depth * wide),
        name="pack_columns",
    )(at, w)


def project_out_kernel(at_ref, near_ref, far_ref, w_ref, w_same_ref, w_cross_ref, *rest):
    out_refs, (w, sems) = rest[:-2], rest[-2:]
    count = len(out_refs)
    tile = out_refs[0].shape[1]
    half = w_same_ref.shape[0]
    core, z, y = at_ref[0], at_ref[1], at_ref[2]
    copies = []
    for n in range(count):
        block = 2 * chip_at(lax.rem(z + (2 * count - 1 - n), count)) + y
        copies.append(
            pltpu.make_async_copy(
                w_ref.at[:, pl.ds(pl.multiple_of(block * tile, tile), tile)], w.at[n], sems.at[n]
            )
        )
    for copy in copies:
        copy.start()
    same = far_ref[:, pl.ds(pl.multiple_of(core * half, half), half)]
    cross = far_ref[:, pl.ds(pl.multiple_of((1 - core) * half, half), half)]
    for n, out_ref in enumerate(out_refs):
        lanes = slice(n * tile, (n + 1) * tile)
        block = jnp.dot(same, w_same_ref[:, lanes], preferred_element_type=F32) + jnp.dot(
            cross, w_cross_ref[:, lanes], preferred_element_type=F32
        )
        copies[n].wait()
        block = block + jnp.dot(near_ref[...], w[n], preferred_element_type=F32)
        out_ref[...] = block.astype(out_ref.dtype)


def project_out(at, near, far, w, w_same, w_cross, count):
    rows, depth = near.shape
    _, wide = w_same.shape
    tile = wide // count
    return pl.pallas_call(
        project_out_kernel,
        in_specs=[SMEM, VMEM, VMEM, ANYWHERE, VMEM, VMEM],
        out_specs=[VMEM] * count,
        out_shape=[sds((rows, tile), BF16)] + [sds((rows, tile), F32)] * (count - 1),
        scratch_shapes=[
            pltpu.VMEM((count, depth, tile), BF16),
            pltpu.SemaphoreType.DMA((count,)),
        ],
        compiler_params=params(),
        cost_estimate=cost(4 * rows * depth * wide, 4 * wide * (rows + depth)),
        name="project_out",
    )(at, near, far, w, w_same, w_cross)


def pair_maps_kernel(sources, first, at_ref, *refs):
    own_ref, other_ref = refs[-2:]
    rows = own_ref.shape[1]
    width = refs[0].shape[1]
    heads = width // HD
    wide = own_ref.shape[2]
    columns = wide // heads
    lane_head = lax.broadcasted_iota(jnp.int32, (columns, width), 1) // HD
    row = lax.broadcasted_iota(jnp.int32, (16, wide), 0)
    column = lax.broadcasted_iota(jnp.int32, (16, wide), 1)
    hit = jnp.zeros((16, wide), jnp.bool_)
    for head in range(heads):
        inside = (column >= head * columns) & (column < (head + 1) * columns)
        hit = hit | (inside & (row >= 3 * head) & (row < 3 * head + 3))
    pick = jnp.where(hit, -1.0, 0.0).astype(BF16)
    straight = (at_ref[2] == at_ref[0]).astype(F32)
    taken = 0
    for place, count in enumerate(sources):
        q_ref, keys = refs[taken], refs[taken + 1 : taken + count]
        taken += count
        if count == 2:
            pieces = [keys[0][n * columns : (n + 1) * columns, :].astype(F32) for n in range(2)]
            levels = keys[0][2 * columns : 2 * columns + 16, first : first + rows]
        else:
            mine = keys[0][0:columns, :].astype(F32)
            theirs = keys[1][0:columns, :].astype(F32)
            pieces = [
                mine * straight + theirs * (1.0 - straight),
                theirs * straight + mine * (1.0 - straight),
            ]
            levels = keys[0][columns : columns + 16, first : first + rows]
        level = lax.dot_general(
            levels, pick, (((0,), (0,)), ((), ())), preferred_element_type=F32
        )
        for k, out_ref in zip(pieces, (own_ref, other_ref)):
            spread = jnp.concatenate(
                [jnp.where(lane_head == head, k, 0.0).astype(BF16) for head in range(heads)], axis=0
            )
            scores = lax.dot_general(
                q_ref[...], spread, (((1,), (1,)), ((), ())), preferred_element_type=F32
            )
            out_ref[place] = jnp.exp((scores + level) * (1.0 / ROOT)).astype(BF16)


def pair_maps(at, sources, columns, first=0):
    rows, width = sources[0][0].shape
    wide = (width // HD) * columns
    count = len(sources)
    flat = [array for source in sources for array in source]
    return pl.pallas_call(
        functools.partial(pair_maps_kernel, [len(source) for source in sources], first),
        in_specs=[SMEM] + [VMEM] * len(flat),
        out_specs=[VMEM] * 2,
        out_shape=[sds((count, rows, wide), BF16)] * 2,
        compiler_params=params(),
        cost_estimate=cost(
            4 * count * rows * wide * width, 8 * count * rows * wide, 2 * count * rows * wide
        ),
        name="pair_maps",
    )(at, *flat)


def pair_kernel(factor, inputs, count, chained, at_ref, *refs):
    maps_refs = refs[:inputs]
    (w_maps_ref, b_maps_ref, gain_ref, bias_ref, w_up_ref, b_up_ref, w_down_ref, b_down_ref) = refs[
        inputs : inputs + 8
    ]
    out_ref, spread_ref, up_ref, shift_ref, rows_ref = refs[inputs + 8 + chained :]
    block = out_ref.shape[0]
    columns = out_ref.shape[1]
    chunk = 8 * columns
    channels = out_ref.shape[2]
    heads_all = w_maps_ref.shape[0]
    heads = heads_all // count
    group = HD // heads_all

    @pl.when(pl.program_id(0) == 0)
    def _():
        row = lax.broadcasted_iota(jnp.int32, (heads_all, heads_all), 0)
        column = lax.broadcasted_iota(jnp.int32, (heads_all, heads_all), 1)
        ring = count // 2
        distance = lax.rem(row // heads, ring)
        chip = chip_at(lax.rem(at_ref[1] + ring - distance, ring))
        side = jnp.where(row // heads >= ring, 1 - at_ref[2], at_ref[2])
        head = (2 * chip + side) * heads + lax.rem(row, heads)
        sort = jnp.where(column == head, 1.0, 0.0).astype(BF16)
        w = jnp.dot(sort, w_maps_ref[...], preferred_element_type=F32)
        w = (w - jnp.sum(w, axis=1, keepdims=True) * (1.0 / channels)) * factor
        high = w.astype(BF16)
        low = (w - high.astype(F32)).astype(BF16)
        spread_ref[...] = jnp.zeros_like(spread_ref)
        for i in range(group):
            at = slice(i * channels, (i + 1) * channels)
            spread_ref[i * heads_all : (i + 1) * heads_all, at] = high
            spread_ref[HD + i * heads_all : HD + (i + 1) * heads_all, at] = low
        b = b_maps_ref[...]
        b = b - jnp.sum(b, axis=1, keepdims=True) * (1.0 / channels)
        shift_ref[...] = jnp.concatenate([b] * group, axis=1)
        up_ref[0:channels, :] = w_up_ref[...]
        b_up = b_up_ref[...]
        top = b_up.astype(BF16).astype(F32)
        middle = (b_up - top).astype(BF16).astype(F32)
        tail = jnp.concatenate(
            [top, middle, b_up - top - middle, jnp.zeros((channels - 3, b_up.shape[1]), F32)], axis=0
        )
        up_ref[channels : 2 * channels, :] = tail.astype(BF16)
        rows_ref[...] = jnp.zeros_like(rows_ref)

    def fill():
        lots = [(ref, n) for ref in maps_refs for n in range(ref.shape[0])]
        for source, (ref, n) in enumerate(lots):
            wide = ref[n].astype(F32)
            for head in range(heads):
                place = (source * heads + head) * block
                rows_ref[place : place + block, 0:columns] = wide[
                    :, head * columns : (head + 1) * columns
                ]

    gain, bias = gain_ref[...], bias_ref[...]

    def normalise(g):
        tall = jnp.concatenate(
            [rows_ref[pl.ds(g * group + i, heads_all, stride=block), :] for i in range(group)], axis=0
        )
        flat = tall.T[0:columns].astype(BF16)
        mixed = (
            jnp.dot(
                jnp.concatenate([flat, flat], axis=1), spread_ref[...], preferred_element_type=F32
            )
            + shift_ref[...]
        )
        pieces = []
        for i in range(group):
            centered = mixed[:, i * channels : (i + 1) * channels]
            variance = jnp.sum(centered * centered, axis=1, keepdims=True) * (1.0 / channels)
            pieces.append((centered * lax.rsqrt(variance + 1e-05) * gain + bias).astype(BF16))
        return jnp.concatenate(pieces, axis=0)

    lane = lax.broadcasted_iota(jnp.int32, (chunk, channels), 1)
    unit = jnp.where(lane < 3, 1.0, 0.0).astype(BF16)

    def transition(normed, at):
        hidden = jnp.dot(
            jnp.concatenate([normed, unit], axis=1), up_ref[...], preferred_element_type=F32
        )
        hidden = jnp.maximum(hidden, 0.0).astype(BF16)
        result = jnp.dot(hidden, w_down_ref[...], preferred_element_type=F32) + b_down_ref[...]
        result = result.astype(BF16)
        for i in range(chunk // columns):
            out_ref[at + i] = result[i * columns : (i + 1) * columns]

    fill()
    per = chunk // columns // group
    waiting = None
    for first in range(0, block // group, per):
        normed = jnp.concatenate([normalise(g) for g in range(first, first + per)], axis=0)
        if waiting is not None:
            transition(*waiting)
        waiting = (normed, first * group)
    transition(*waiting)


def pair_block_fast(
    at,
    maps,
    w_maps,
    b_maps,
    pair_gain,
    pair_bias,
    w_up,
    b_up,
    w_down,
    b_down,
    factor,
    columns,
    block=64,
    first=0,
    blocks=None,
    begun=None,
):
    count = sum(array.shape[0] for array, _ in maps)
    rows, wide = maps[0][0].shape[1:]
    channels, hidden = w_up.shape
    heads_all = w_maps.shape[0]
    group = HD // heads_all
    whole = lambda *shape: pl.BlockSpec(shape, lambda n: (0,) * len(shape))
    blocks = rows // block if blocks is None else blocks
    pairs = blocks * block * columns
    chained = [] if begun is None else [begun]
    return pl.pallas_call(
        functools.partial(pair_kernel, factor, len(maps), count, len(chained)),
        grid=(blocks,),
        in_specs=[SMEM]
        + [
            pl.BlockSpec(
                (array.shape[0], block, wide),
                lambda n, skipped=skipped: (0, first + n - skipped // block, 0),
            )
            for array, skipped in maps
        ]
        + [
            whole(heads_all, channels),
            whole(1, channels),
            whole(1, channels),
            whole(1, channels),
            whole(channels, hidden),
            whole(1, hidden),
            whole(hidden, channels),
            whole(1, channels),
        ]
        + [pl.BlockSpec(memory_space=pl.ANY)] * len(chained),
        out_specs=pl.BlockSpec((block, columns, channels), lambda n: (first + n, 0, 0)),
        out_shape=sds((rows, columns, channels), BF16),
        scratch_shapes=[
            pltpu.VMEM((2 * HD, group * channels), BF16),
            pltpu.VMEM((2 * channels, hidden), BF16),
            pltpu.VMEM((1, group * channels), F32),
            pltpu.VMEM((heads_all * block, HD), F32),
        ],
        input_output_aliases={len(maps) + 9: 0} if chained else {},
        compiler_params=params("arbitrary"),
        cost_estimate=cost(4 * pairs * channels * hidden, 4 * pairs * channels, pairs * channels),
        name="pair_block",
    )(
        at,
        *[array for array, _ in maps],
        w_maps,
        b_maps.reshape(1, -1),
        pair_gain.reshape(1, -1),
        pair_bias.reshape(1, -1),
        w_up,
        b_up.reshape(1, -1),
        w_down,
        b_down.reshape(1, -1),
        *chained,
    )


def per_device_fast(
    layer_input,
    norm_gain,
    norm_bias,
    w_query_key,
    w_value,
    w_out,
    w_maps,
    b_maps,
    pair_gain,
    pair_bias,
    w_up,
    b_up,
    w_down,
    b_down,
):
    rows = layer_input.shape[0]
    parts = lax.axis_size("mp")
    ring = parts // 2
    tokens = rows * lax.axis_size("rows")
    columns = tokens // parts
    core = lax.axis_index("rows")
    z, y = lax.axis_index("mp") // 2, lax.axis_index("mp") % 2

    swap_core = [(0, 1), (1, 0)]
    swap_y = [(m, m ^ 1) for m in range(parts)]

    def rotate_z(by):
        chips = [a ^ (a >> 1) for a in range(ring)]
        return [
            (2 * chips[a] + b, 2 * chips[(a + by) % ring] + b) for a in range(ring) for b in range(2)
        ]

    half = HD // 2
    freqs = 10000.0 ** (-jnp.arange(half, dtype=F32) / half)
    positions = core * rows + jnp.arange(rows, dtype=jnp.int32)
    angles = positions.astype(F32)[:, None] * freqs[None, :]
    at = jnp.stack([core, chip_at(z), y]).astype(jnp.int32)

    w_half = pack_columns(at, w_out, ring)
    w_same = lax.ppermute(w_half, "mp", swap_y)
    queries, own = project(
        layer_input, norm_gain, norm_bias, w_query_key, w_value, jnp.cos(angles), jnp.sin(angles)
    )
    there = lax.ppermute(own, "rows", swap_core)
    passed = [queries]
    for _ in range(1, ring - 1):
        passed.append(lax.ppermute(passed[-1], "mp", rotate_z(1)))
    calls = 3
    cut = rows // calls
    last = [lax.ppermute(part, "mp", rotate_z(1)) for part in (passed[-1][:cut], passed[-1][cut:])]
    near, local, *shares = attend(at, queries, own, there, ring, columns)
    sources = [(queries, local)]
    for d in range(1, ring):
        mine = lax.ppermute(shares[d - 1], "mp", rotate_z(d))
        theirs = lax.ppermute(mine, "rows", swap_core)
        if d < ring - 1:
            sources.append((passed[d], mine, theirs))
    far = lax.ppermute(near, "mp", swap_y)
    w_cross = lax.ppermute(w_same, "rows", swap_core)

    own_maps, other_maps = [], []
    for some, start in (
        (sources[:-1], 0),
        (sources[-1:], 0),
        ([(last[0], mine, theirs)], 0),
        ([(last[1], mine, theirs)], cut),
    ):
        own_side, other_side = pair_maps(at, some, columns, start)
        own_maps.append((own_side, start))
        other_maps.append((lax.ppermute(other_side, "mp", swap_y), start))

    total, *tails = project_out(at, near, far, w_out, w_same, w_cross, ring)
    pair = functools.partial(
        pair_block_fast,
        at,
        w_maps=w_maps,
        b_maps=b_maps,
        pair_gain=pair_gain,
        pair_bias=pair_bias,
        w_up=w_up,
        b_up=b_up,
        w_down=w_down,
        b_down=b_down,
        factor=float(tokens),
        columns=columns,
    )
    for tail in tails:
        sent = total.astype(BF16)
        total = tail + lax.ppermute(sent, "mp", rotate_z(1)).astype(F32)
    attention = total
    blocks = rows // 64
    pair_features = None
    for n in range(calls):
        pair_features = pair(
            [side[k] for side in (own_maps, other_maps) for k in (0, 1, 2 if n == 0 else 3)],
            first=n * blocks // calls,
            blocks=blocks // calls,
            begun=pair_features,
        )
    return (attention, pair_features)


def layer_norm(values, gain, bias):
    average = jnp.mean(values, axis=-1, keepdims=True)
    centered = values - average
    variance = jnp.mean(centered * centered, axis=-1, keepdims=True)
    return centered * lax.rsqrt(variance + 1e-05) * gain + bias


def rotate(values, positions):
    half = values.shape[-1] // 2
    freqs = 10000.0 ** (-jnp.arange(half, dtype=jnp.float32) / half)
    angles = positions.astype(jnp.float32)[:, None] * freqs[None, :]
    cosine = jnp.cos(angles)[:, None, :]
    sine = jnp.sin(angles)[:, None, :]
    lower = values[..., :half]
    upper = values[..., half:]
    return jnp.concatenate([lower * cosine - upper * sine, upper * cosine + lower * sine], axis=-1)


def project_rotated(normed, weight, positions):
    count = normed.shape[0]
    projected = jnp.dot(normed, weight, preferred_element_type=jnp.float32)
    projected = projected.reshape(count, weight.shape[1] // HD, HD)
    return rotate(projected, positions).astype(jnp.bfloat16).reshape(count, weight.shape[1])


def pair_block(maps, w_maps, b_maps, pair_gain, pair_bias, w_up, b_up, w_down, b_down, factor):
    mixed = (
        jnp.einsum("hrc,hp->rcp", maps, w_maps, preferred_element_type=jnp.float32) * factor
        + b_maps
    )
    normed = layer_norm(mixed, pair_gain, pair_bias).astype(jnp.bfloat16)
    hidden = jax.nn.relu(
        jnp.einsum("rcp,pt->rct", normed, w_up, preferred_element_type=jnp.float32) + b_up
    ).astype(jnp.bfloat16)
    return (
        jnp.einsum("rct,tp->rcp", hidden, w_down, preferred_element_type=jnp.float32) + b_down
    ).astype(jnp.bfloat16)


def per_device(
    layer_input,
    norm_gain,
    norm_bias,
    w_query_key,
    w_value,
    w_out,
    w_maps,
    b_maps,
    pair_gain,
    pair_bias,
    w_up,
    b_up,
    w_down,
    b_down,
):
    tok_rows = layer_input.shape[0]
    tokens_all = tok_rows * lax.axis_size("rows")
    local_heads = w_value.shape[1] // HD
    normed = layer_norm(layer_input.astype(jnp.float32), norm_gain, norm_bias).astype(jnp.bfloat16)
    own_positions = lax.axis_index("rows") * tok_rows + jnp.arange(tok_rows, dtype=jnp.int32)
    queries = project_rotated(normed, w_query_key[0], own_positions)
    keys_local = project_rotated(normed, w_query_key[1], own_positions)
    values_local = jnp.dot(normed, w_value, preferred_element_type=jnp.float32).astype(jnp.bfloat16)
    keys_all, values_all = (
        lax.all_gather(keys_local, "rows", axis=0, tiled=True),
        lax.all_gather(values_local, "rows", axis=0, tiled=True),
    )
    head_queries = queries.reshape(tok_rows, local_heads, HD)
    head_keys = keys_all.reshape(tokens_all, local_heads, HD)
    head_values = values_all.reshape(tokens_all, local_heads, HD)
    scores = jnp.einsum(
        "qhd,khd->hqk", head_queries, head_keys, preferred_element_type=jnp.float32
    ) / math.sqrt(HD)
    maps = jax.nn.softmax(scores, axis=-1).astype(jnp.bfloat16)
    context = jnp.einsum("hqk,khd->qhd", maps, head_values, preferred_element_type=jnp.float32)
    context = context.astype(jnp.bfloat16).reshape(tok_rows, local_heads * HD)
    partial_sums = jnp.dot(context, w_out, preferred_element_type=jnp.float32)
    attention = lax.psum_scatter(partial_sums, "mp", scatter_dimension=1, tiled=True)
    factor = float(tokens_all)
    pair_features = pair_block(
        lax.all_to_all(maps, "mp", split_axis=2, concat_axis=0, tiled=True),
        w_maps,
        b_maps,
        pair_gain,
        pair_bias,
        w_up,
        b_up,
        w_down,
        b_down,
        factor,
    )
    return (attention, pair_features)


def solution(mesh):
    in_specs = (
        P(("groups", "rows"), None),
        P(),
        P(),
        P(None, None, "mp"),
        P(None, "mp"),
        P("mp", None),
        P(),
        P(),
        P(),
        P(),
        P(),
        P(),
        P(),
        P(),
    )
    out_specs = (P(("groups", "rows"), "mp"), P(("groups", "rows"), "mp", None))
    if mesh.shape["mp"] != 8 or mesh.shape["rows"] != 2:
        return jax.shard_map(
            per_device, mesh=mesh, in_specs=in_specs, out_specs=out_specs, check_vma=False
        )

    return jax.shard_map(
        per_device_fast, mesh=mesh, in_specs=in_specs, out_specs=out_specs, check_vma=False
    )
```
